32 devices in a mesh: node: 2 (over x), rep: 4 (over y, core), feat: 4 (over z).
Axes of the slice: x: 2, y: 2, z: 4, core: 2. Of those that a mesh axis runs over, the one named last changes fastest.
Arguments:
- cotangent: bfloat16 [256, 8192], P('feat', ('node', 'rep')), may hold values from -6 to 6
- preact: bfloat16 [256, 8192], P('feat', ('node', 'rep')), may hold values from -6 to 6
- features: bfloat16 [256, 8192], P(None, ('node', 'rep', 'feat')), may hold values from -6 to 6
- weight: bfloat16 [256, 256], replicated, may hold values from -0.375 to 0.375
- tile_values: bfloat16 [2, 2, 4, 4, 128, 128], P('node', None, 'rep'), may hold values from -0.5 to 0.5
- source_blocks: int32 [2, 2, 4, 4], P('node', None, 'rep'), may hold values from 0 to 7
- target_blocks: int32 [2, 2, 4, 4], P('node', None, 'rep'), may hold values from 0 to 31
- tile_counts: int32 [2, 2, 4], P('node', None, 'rep'), may hold values from 0 to 4, as said below
Outputs:
- input_grad: bfloat16 [256, 8192], P(None, ('node', 'rep', 'feat'))
- weight_grad: float32 [256, 256], replicated
The draws below stay inside these ranges and needn't reach their ends.
Inputs may be any that keep to these rules, and one draw needn't show every extreme that they name: For every target group i and piece k some source group s has tile_counts[i, s, k] equal to 4.
All inputs are finite; a program needn't handle non-finite values.
Results may differ from the reference program's by a relative error of at most 0.0049.
Values may be sent and summed in bfloat16 or wider, within the bound.
A program may use at most 64 MiB of HBM per device.

```python
import math
import jax
import jax.numpy as jnp
from jax import lax

F = 256
BLOCK = 128
BLK_DEV = 8
TILES = 4
NODES = 8192
N_NODE = 2
N_REP = 4


def draw_tile_counts(key, part):
    level_key = jax.random.fold_in(key, 11)
    section_key = jax.random.fold_in(key, 23)
    levels = jnp.array([TILES, TILES // 2, TILES // 4, 0], dtype=jnp.int32)
    level_pick = jax.random.randint(level_key, (N_NODE, N_NODE, N_REP), 0, 4)
    counts = levels[level_pick]
    full_section = jax.random.randint(section_key, (N_NODE, 1, N_REP), 0, N_NODE)
    section_ids = jnp.arange(N_NODE, dtype=jnp.int32)[None, :, None]
    return jnp.where(section_ids == full_section, TILES, counts).astype(jnp.int32)


def set_ends(entries, rng, least, largest):
    index_at = [jax.random.randint(jax.random.fold_in(rng, axis), (), 0, length) for axis, length in enumerate(entries.shape)]
    longest = entries.shape.index(max(entries.shape))
    next_to = index_at[:longest] + [(index_at[longest] + 1) % entries.shape[longest]] + index_at[longest + 1:]
    return entries.at[tuple(index_at)].set(least).at[tuple(next_to)].set(largest)


def shard_levels(stream_key, dims, cuts, smallest, largest):
    level, own = 1.0, jax.random.fold_in(stream_key, 6)
    for position, shards_of in cuts:
        heights = jnp.exp(jax.random.uniform(jax.random.fold_in(own, position), (shards_of,), jnp.float32, smallest / len(cuts), largest / len(cuts)))
        level = level * jnp.repeat(heights, dims[position] // shards_of).reshape([-1 if axis == position else 1 for axis in range(len(dims))])
    return level


def bell_draw(stream_key, shape, spread, most, split=(), kind=jnp.bfloat16):
    values = spread * jax.random.normal(stream_key, shape, jnp.float32)
    if split:
        values = values * shard_levels(stream_key, shape, split, -0.22, 0.18)
    return jnp.clip(values, -most, most).astype(kind)


def setup_inputs(seed: int = 0) -> dict:
    arg_keys = jax.random.split(jax.random.key(seed), 9)
    return {
        "cotangent": bell_draw(arg_keys[0], (F, NODES), 1.0, 6.0, ((0, 4), (1, 8))),
        "preact": bell_draw(arg_keys[1], (F, NODES), 1.0, 6.0, ((0, 4), (1, 8))),
        "features": bell_draw(arg_keys[2], (F, NODES), 1.0, 6.0, ((1, 32),)),
        "weight": bell_draw(arg_keys[3], (F, F), F ** -0.5, 0.375),
        "tile_values": bell_draw(arg_keys[4], (N_NODE, N_NODE, N_REP, TILES, BLOCK, BLOCK), (BLOCK * max(1, 7 * N_NODE // (4 * BLK_DEV))) ** -0.5, 0.5, ((0, 2), (2, 4))),
        "source_blocks": set_ends(jax.random.randint(arg_keys[5], (N_NODE, N_NODE, N_REP, TILES), 0, BLK_DEV), jax.random.fold_in(arg_keys[5], 1), 0, BLK_DEV - 1).astype(jnp.int32),
        "target_blocks": set_ends(jax.random.randint(arg_keys[6], (N_NODE, N_NODE, N_REP, TILES), 0, N_REP * BLK_DEV), jax.random.fold_in(arg_keys[6], 1), 0, (N_REP * BLK_DEV) - 1).astype(jnp.int32),
        "tile_counts": draw_tile_counts(jax.random.fold_in(arg_keys[8], 71), 0),
    }


def reference(cotangent, preact, features, weight, tile_values, source_blocks, target_blocks, tile_counts):
    grad_pre = jnp.where(preact > 0, cotangent, jnp.zeros_like(cotangent))
    dest_count = N_REP * BLK_DEV
    grad_grid = grad_pre.reshape(F, N_NODE, N_REP, BLK_DEV, BLOCK)
    section_index = jnp.arange(N_NODE, dtype=jnp.int32)[:, None, None] * jnp.ones((1, N_REP, TILES), jnp.int32)
    piece_index = jnp.arange(N_REP, dtype=jnp.int32)[None, :, None] * jnp.ones((N_NODE, 1, TILES), jnp.int32)
    slot_index = jnp.arange(TILES, dtype=jnp.int32)
    target_index = jnp.arange(dest_count, dtype=jnp.int32)

    def one_group(group):
        values, sources, targets, counts = group
        picked = grad_grid[:, section_index, piece_index, sources, :].astype(jnp.float32)
        products = jnp.einsum('fsktb,sktbc->fsktc', picked, values.astype(jnp.float32), precision=lax.Precision.HIGHEST)
        alive = (slot_index[None, None, :] < counts[:, :, None]).astype(jnp.float32)
        onehot = (targets[..., None] == target_index[None, None, None, :]).astype(jnp.float32) * alive[..., None]
        summed = jnp.einsum('fsktc,sktg->fgc', products, onehot, precision=lax.Precision.HIGHEST)
        return summed.reshape(F, dest_count * BLOCK)
    grouped = lax.map(one_group, (tile_values, source_blocks, target_blocks, tile_counts))
    agg_grad = jnp.transpose(grouped, (1, 0, 2)).reshape(F, NODES).astype(jnp.bfloat16)
    input_grad = jnp.dot(weight, agg_grad, preferred_element_type=jnp.float32).astype(jnp.bfloat16)
    grad_scale = 1.0 / math.sqrt(NODES)
    weight_grad = lax.dot_general(features, agg_grad, (((1,), (1,)), ((), ())), preferred_element_type=jnp.float32) * grad_scale
    return (input_grad, weight_grad)
```

```python
import functools
import math

import jax
import jax.numpy as jnp
from jax import lax
from jax.experimental import pallas as pl
from jax.experimental.pallas import tpu as pltpu
from jax.sharding import PartitionSpec as P

MESH = pl.DeviceIdType.MESH
BLOCK = 128
CHUNKS = 4
ROWS = 16
SUBS = 4
MAX_SENDS = 32


def kernel(
    groups, pieces, shards,
    cot_hbm, pre_hbm, feat_hbm, tiles_hbm, source_ref, target_ref, count_ref,
    stacked_ref, all_ref,
    cot, pre, tiles, own_grad, grads, feats, tgt, own_prod, prod_a, prod_b, acc, aggs, agg_all,
    wt_own, rs_send, rs_recv, ag_send, gathered,
    load_sem, x_ss, x_rs, f_ss, f_rs, t_ss, t_rs, a_ss, a_rs, b_ss, b_rs, z_ss, z_rs, r_ss, r_rs, g_ss, g_rs,
):
    node = lax.axis_index("node")
    rep = lax.axis_index("rep")
    feat = lax.axis_index("feat")
    devices = groups * pieces * shards
    plane = groups * pieces
    me = (node * pieces + rep) * shards + feat
    slots = tiles_hbm.shape[3]
    width = cot.shape[0]
    piece_len = cot.shape[1]
    chunk = width // CHUNKS
    blocks = piece_len // BLOCK
    cols = piece_len // shards
    in_feats = feats.shape[1]
    halves = in_feats // BLOCK
    parts = (width // ROWS) * halves

    def copy(src, dst, ss, rs, **where):
        where = {"node": node, "rep": rep, "feat": feat, **where}
        return pltpu.make_async_remote_copy(
            src_ref=src, dst_ref=dst, send_sem=ss, recv_sem=rs, device_id=where, device_id_type=MESH
        )

    def flip(index, mask):
        bit = 1
        while bit <= mask:
            if mask & bit:
                index = index + bit * (1 - 2 * lax.rem(index // bit, 2))
            bit *= 2
        return index

    powers = all(n & (n - 1) == 0 for n in (groups, pieces, shards))
    flips = sorted(
        ((z, n, r) for z in range(shards) for n in range(groups) for r in range(pieces) if z or n or r),
        key=lambda f: (-f[0], -(f[1] > 0) - (f[2] > 1)))

    def peer_of(off):
        peer = lax.rem(me + off, devices)
        return {
            "node": peer // (pieces * shards),
            "rep": lax.rem(peer // shards, pieces),
            "feat": lax.rem(peer, shards),
        }

    barrier = pltpu.get_barrier_semaphore()

    def greet(**where):
        where = {"node": node, "rep": rep, "feat": feat, **where}
        pl.semaphore_signal(barrier, inc=1, device_id=where, device_id_type=MESH)

    for off in range(1, groups):
        greet(node=lax.rem(node + off, groups))
    for off in range(1, pieces):
        greet(rep=lax.rem(rep + off, pieces))
    pl.when(feat < shards - 1)(lambda: greet(feat=feat + 1))
    pl.when(feat > 0)(lambda: greet(feat=feat - 1))

    loads = [
        pltpu.make_async_copy(cot_hbm, cot, load_sem.at[0]),
        pltpu.make_async_copy(pre_hbm, pre, load_sem.at[1]),
        pltpu.make_async_copy(feat_hbm, feats.at[feat], load_sem.at[2]),
        pltpu.make_async_copy(tiles_hbm, tiles, load_sem.at[3]),
    ]
    for load in loads:
        load.start()
    loads[0].wait()
    loads[1].wait()
    for h in range(CHUNKS):
        rows = pl.ds(h * chunk, chunk)
        for d in range(blocks):
            c = cot[rows, pl.ds(d * BLOCK, BLOCK)]
            own_grad[h, d] = jnp.where(pre[rows, pl.ds(d * BLOCK, BLOCK)] > 0, c, jnp.zeros_like(c))
    for g in range(groups):
        s = lax.rem(node - g + groups, groups)
        for t in range(slots):
            count = jnp.full((1, BLOCK), count_ref[s], jnp.int32)
            target = jnp.full((1, BLOCK), target_ref[0, s, 0, t], jnp.int32)
            tgt[0, pl.ds(g * slots + t, 1), :] = jnp.where(count > t, target, jnp.full_like(target, -1))
    ends = jnp.where(feat == 0, 1, 0) + jnp.where(feat == shards - 1, 1, 0)
    pl.semaphore_wait(barrier, groups + pieces - ends)

    sends = []
    for h in range(CHUNKS):
        for off in range(1, groups):
            sends.append(copy(
                own_grad.at[h], grads[h].at[off - 1], x_ss.at[h, off], x_rs.at[h, off],
                node=lax.rem(node + off, groups)))
            sends[-1].start()

    def relay(step, sub, block, to):
        rows = pl.ds(sub * (in_feats // SUBS), in_feats // SUBS)
        way = 0 if to > 0 else 1
        part = feats.at[block, rows]
        return copy(part, part, f_ss.at[way, step, sub], f_rs.at[way, step, sub], feat=feat + to)

    def outgoing(step, sub, act):
        for to, ok in ((1, feat < shards - 1), (-1, feat > 0)):
            block = feat - to * step

            @pl.when(ok & (block >= 0) & (block < shards))
            def _():
                act(relay(step, sub, block, to))

    def pass_on(step, sub):
        outgoing(step, sub, lambda c: c.start())

    def settle(step, sub):
        outgoing(step, sub, lambda c: c.wait_send())

    def arrive(step, sub):
        for to in (1, -1):
            block = feat - to * (step + 1)

            @pl.when((block >= 0) & (block < shards))
            def _():
                relay(step, sub, block, to).wait_recv()

    todo = [(step, sub) for step in range(shards - 1) for sub in range(SUBS)]

    def forward(count):
        for step, sub in todo[:count]:
            arrive(step, sub)
            if step < shards - 2:
                pass_on(step + 1, sub)
        del todo[:count]

    loads[2].wait()
    for sub in range(SUBS):
        pass_on(0, sub)

    loads[3].wait()
    for t in range(slots):
        block = source_ref[0, node, 0, t]
        picked = jnp.concatenate([own_grad[h, block] for h in range(CHUNKS)], axis=0)
        out = jnp.dot(picked, tiles[0, node, 0, t], preferred_element_type=jnp.float32)
        for h in range(CHUNKS):
            part = out[h * chunk:(h + 1) * chunk]
            own_prod[h, t] = part
            prod_a[0, h, t] = part.astype(jnp.bfloat16)
    for off in range(1, pieces):
        to = lax.rem(rep + off, pieces)
        sends.append(copy(tgt.at[0], tgt.at[off], t_ss.at[off], t_rs.at[off], rep=to))
        sends[-1].start()
        sends.append(copy(prod_a.at[0], prod_a.at[off], a_ss.at[off], a_rs.at[off], rep=to))
        sends[-1].start()

    def other_products(h, off):
        s = lax.rem(node - off + groups, groups)
        for t in range(slots):
            out = jnp.dot(grads[h][off - 1, source_ref[0, s, 0, t]], tiles[0, s, 0, t],
                          preferred_element_type=jnp.float32)
            own_prod[h, off * slots + t] = out
            prod_b[0, h, (off - 1) * slots + t] = out.astype(jnp.bfloat16)

    for h in range(CHUNKS):
        for off in range(1, groups):
            copy(own_grad.at[h], grads[h].at[off - 1], x_ss.at[h, off], x_rs.at[h, off]).wait_recv()
        if groups <= 4:
            for off in range(1, groups):
                other_products(h, off)
        else:
            lax.fori_loop(1, groups, lambda off, carry, h=h: (other_products(h, off), carry)[1], 0)
        for off in range(1, pieces):
            sends.append(copy(
                prod_b.at[0, h], prod_b.at[off, h], b_ss.at[h, off], b_rs.at[h, off],
                rep=lax.rem(rep + off, pieces)))
            sends[-1].start()
        forward(SUBS // CHUNKS)

    def add_up(total, from_rep, first, count, read):
        def step(n, total):
            value = read(n).astype(jnp.float32)
            to = tgt[from_rep, pl.ds(first + n, 1), :]
            zero = jnp.zeros_like(value)
            return tuple(
                part + jnp.where(jnp.broadcast_to(to == rep * blocks + d, value.shape), value, zero)
                for d, part in enumerate(total)
            )

        return lax.fori_loop(0, count, step, total, unroll=count <= 8)

    def add_near(h):
        total = tuple(jnp.zeros((chunk, BLOCK), jnp.float32) for _ in range(blocks))
        total = add_up(total, 0, 0, groups * slots, lambda n: own_prod[h, n])
        for off in range(1, pieces):
            total = add_up(total, off, 0, slots, lambda n, off=off: prod_a[off, h, n])
        for d in range(blocks):
            acc[h, d] = total[d]

    for off in range(1, pieces):
        copy(tgt.at[0], tgt.at[off], t_ss.at[off], t_rs.at[off]).wait_recv()
        copy(prod_a.at[0], prod_a.at[off], a_ss.at[off], a_rs.at[off]).wait_recv()
    for h in range(CHUNKS):
        add_near(h)

    per = cols // BLOCK
    for h in range(CHUNKS):
        forward(SUBS // CHUNKS)
        for off in range(1, pieces):
            copy(prod_b.at[0, h], prod_b.at[off, h], b_ss.at[h, off], b_rs.at[h, off]).wait_recv()
        total = tuple(acc[h, d] for d in range(blocks))
        for off in range(1, pieces):
            total = add_up(
                total, off, slots, (groups - 1) * slots, lambda n, h=h, off=off: prod_b[off, h, n])
        for d in range(blocks):
            aggs[d // per, pl.ds(h * chunk, chunk), pl.ds((d % per) * BLOCK, BLOCK)] = total[d].astype(jnp.bfloat16)
    agg_all[feat] = aggs[feat]

    forward(len(todo))
    scale = 1.0 / math.sqrt(piece_len * plane)
    wt = jnp.zeros((width, in_feats), jnp.float32)
    for z in range(shards):
        wt += lax.dot_general(
            aggs[z], feats[z], (((1,), (1,)), ((), ())), preferred_element_type=jnp.float32)
    wt *= scale
    for p in range(parts):
        part = wt[(p // halves) * ROWS:(p // halves + 1) * ROWS, (p % halves) * BLOCK:(p % halves + 1) * BLOCK]
        wt_own[p] = part
        rs_send[p] = part.astype(jnp.bfloat16)

    place = node * pieces + rep

    def to_reducer(q):
        return copy(
            rs_send.at[q], rs_recv.at[lax.rem(place - q + plane, plane)], r_ss.at[q], r_rs,
            node=q // pieces, rep=lax.rem(q, pieces))

    if plane == parts:
        for off in range(1, plane):
            sends.append(to_reducer(lax.rem(place + off, plane)))
            sends[-1].start()
    else:
        for q in range(parts):
            @pl.when(place != q)
            def _():
                to_reducer(q).start()

    for off in range(1, shards):
        to = lax.rem(feat + off, shards)
        sends.append(copy(aggs.at[to], agg_all.at[feat], z_ss.at[off], z_rs.at[off], feat=to))
        sends[-1].start()

    def reduce_and_send():
        pltpu.make_async_copy(
            rs_recv.at[pl.ds(1, plane - 1)], rs_recv.at[pl.ds(1, plane - 1)], r_rs).wait()
        total = lax.fori_loop(
            1, plane, lambda j, value: value + rs_recv[j].astype(jnp.float32), wt_own[place],
            unroll=plane <= 8)
        ag_send[...] = total.astype(jnp.bfloat16)
        mine = feat * parts + place
        gathered[mine] = ag_send[...]

        if powers and devices <= MAX_SENDS:
            for off, (z, n, r) in enumerate(flips, 1):
                copy(ag_send, gathered.at[mine], g_ss.at[off], g_rs,
                     node=flip(node, n), rep=flip(rep, r), feat=flip(feat, z)).start()
            return

        def send(off, carry):
            if devices - 1 > MAX_SENDS:
                @pl.when(off > MAX_SENDS)
                def _():
                    copy(ag_send, gathered.at[mine], g_ss.at[lax.rem(off, MAX_SENDS)], g_rs).wait_send()
            copy(ag_send, gathered.at[mine], g_ss.at[lax.rem(off, MAX_SENDS)], g_rs,
                 **peer_of(off)).start()
            return carry

        lax.fori_loop(1, devices, send, 0)

    if plane == parts:
        reduce_and_send()
    else:
        pl.when(place < parts)(reduce_and_send)

    for off in range(1, shards):
        origin = lax.rem(feat - off + shards, shards)
        copy(aggs.at[0], agg_all.at[origin], z_ss.at[off], z_rs.at[off]).wait_recv()

    stacked_ref[...] = agg_all[...].reshape(shards * width, cols)

    def all_but(k):
        pltpu.make_async_copy(gathered.at[pl.ds(0, shards * parts - k)],
                              gathered.at[pl.ds(0, shards * parts - k)], g_rs).wait()

    if plane == parts:
        all_but(1)
    else:
        pl.when(place < parts)(lambda: all_but(1))
        pl.when(place >= parts)(lambda: all_but(0))
    all_ref[...] = gathered[...]

    def drain():
        def wait(off, carry):
            copy(ag_send, gathered.at[0], g_ss.at[lax.rem(off, MAX_SENDS)], g_rs).wait_send()
            return carry

        lax.fori_loop(max(1, devices - MAX_SENDS), devices, wait, 0)

    if plane == parts:
        drain()
    else:
        pl.when(place < parts)(drain)
        for q in range(parts):
            @pl.when(place != q)
            def _():
                to_reducer(q).wait_send()
    for step in range(shards - 1):
        for sub in range(SUBS):
            settle(step, sub)
    for sent in sends:
        sent.wait_send()


def finish(halves, weight_ref, stacked_ref, all_ref, ig_ref, wg_ref):
    ig_ref[...] = jnp.dot(
        weight_ref[...], stacked_ref[...], preferred_element_type=jnp.float32).astype(jnp.bfloat16)
    bands = all_ref.shape[0] // halves
    for half in range(halves):
        side = jnp.concatenate([all_ref[b * halves + half] for b in range(bands)], axis=0)
        wg_ref[pl.ds(half * BLOCK, BLOCK), :] = side.astype(jnp.float32).T


def shards_step(groups, pieces, shards, cotangent, preact, features, weight, tile_values,
                source_blocks, target_blocks, tile_counts):
    width, piece_len = cotangent.shape
    slots = tile_values.shape[3]
    chunk = width // CHUNKS
    blocks = piece_len // BLOCK
    cols = piece_len // shards
    in_feats = features.shape[0]
    plane = groups * pieces
    parts = (width // ROWS) * (in_feats // BLOCK)
    bf16, f32 = jnp.bfloat16, jnp.float32
    dma = pltpu.SemaphoreType.DMA
    hbm = pl.BlockSpec(memory_space=pl.ANY)
    smem = pl.BlockSpec(memory_space=pltpu.SMEM)
    vmem = pl.BlockSpec(memory_space=pltpu.VMEM)
    stacked, everything = pl.pallas_call(
        functools.partial(kernel, groups, pieces, shards),
        out_shape=(
            jax.ShapeDtypeStruct((width * shards, cols), bf16),
            jax.ShapeDtypeStruct((shards * parts, ROWS, BLOCK), bf16),
        ),
        in_specs=[hbm] * 4 + [smem] * 3,
        out_specs=(vmem, vmem),
        scratch_shapes=[
            pltpu.VMEM((width, piece_len), bf16),
            pltpu.VMEM((width, piece_len), bf16),
            pltpu.VMEM(tile_values.shape, bf16),
            pltpu.VMEM((CHUNKS, blocks, chunk, BLOCK), bf16),
            [pltpu.VMEM((max(groups - 1, 1), blocks, chunk, BLOCK), bf16) for _ in range(CHUNKS)],
            pltpu.VMEM((shards, in_feats, cols), bf16),
            pltpu.VMEM((pieces, groups * slots, BLOCK), jnp.int32),
            pltpu.VMEM((CHUNKS, groups * slots, chunk, BLOCK), f32),
            pltpu.VMEM((pieces, CHUNKS, slots, chunk, BLOCK), bf16),
            pltpu.VMEM((pieces, CHUNKS, (groups - 1) * slots, chunk, BLOCK), bf16),
            pltpu.VMEM((CHUNKS, blocks, chunk, BLOCK), f32),
            pltpu.VMEM((shards, width, cols), bf16),
            pltpu.VMEM((shards, width, cols), bf16),
            pltpu.VMEM((parts, ROWS, BLOCK), f32),
            pltpu.VMEM((parts, ROWS, BLOCK), bf16),
            pltpu.VMEM((plane, ROWS, BLOCK), bf16),
            pltpu.VMEM((ROWS, BLOCK), bf16),
            pltpu.VMEM((shards * parts, ROWS, BLOCK), bf16),
            dma((4,)),
            dma((CHUNKS, groups)), dma((CHUNKS, groups)),
            dma((2, shards, SUBS)), dma((2, shards, SUBS)),
            dma((pieces,)), dma((pieces,)),
            dma((pieces,)), dma((pieces,)),
            dma((CHUNKS, pieces)), dma((CHUNKS, pieces)),
            dma((shards,)), dma((shards,)),
            dma((parts,)), dma(()),
            dma((MAX_SENDS,)), dma(()),
        ],
        compiler_params=pltpu.CompilerParams(collective_id=0, has_side_effects=True),
        name="graph_backward",
    )(cotangent, preact, features, tile_values, source_blocks, target_blocks, tile_counts.reshape(groups))
    return pl.pallas_call(
        functools.partial(finish, in_feats // BLOCK),
        out_shape=(
            jax.ShapeDtypeStruct((weight.shape[0], cols), bf16),
            jax.ShapeDtypeStruct((in_feats, width * shards), f32),
        ),
        in_specs=[vmem] * 3,
        out_specs=(vmem, vmem),
        name="finish",
    )(weight, stacked, everything)


def solution(mesh):
    step = functools.partial(shards_step, mesh.shape["node"], mesh.shape["rep"], mesh.shape["feat"])
    in_specs = (
        P("feat", ("node", "rep")),
        P("feat", ("node", "rep")),
        P(None, ("node", "rep", "feat")),
        P(),
        P("node", None, "rep", None, None, None),
        P("node", None, "rep", None),
        P("node", None, "rep", None),
        P("node", None, "rep"),
    )
    out_specs = (P(None, ("node", "rep", "feat")), P())
    return jax.shard_map(step, mesh=mesh, in_specs=in_specs, out_specs=out_specs, check_vma=False)
```

```python
import functools
import math

import jax
import jax.numpy as jnp
from jax import lax
from jax.experimental import pallas as pl
from jax.experimental.pallas import tpu as pltpu
from jax.sharding import PartitionSpec as P

MESH = pl.DeviceIdType.MESH
BLOCK = 128
CHUNKS = 4
ROWS = 16
SUBS = 4
MAX_SENDS = 32


def kernel(
    groups, pieces, shards,
    cot_hbm, pre_hbm, feat_hbm, tiles_hbm, source_hbm, target_hbm, count_hbm,
    stacked_ref, all_ref,
    cot, pre, tiles, own_grad, grads, feats, tgt, own_prod, prod_a, prod_b, acc, aggs, agg_all,
    wt_own, rs_send, rs_recv, ag_send, gathered, source_ref, target_ref, count_ref,
    load_sem, x_ss, x_rs, f_ss, f_rs, t_ss, t_rs, a_ss, a_rs, b_ss, b_rs, z_ss, z_rs, r_ss, r_rs, g_ss, g_rs,
):
    node = lax.axis_index("node")
    rep = lax.axis_index("rep")
    feat = lax.axis_index("feat")
    devices = groups * pieces * shards
    plane = groups * pieces
    me = (node * pieces + rep) * shards + feat
    slots = tiles_hbm.shape[3]
    width = cot.shape[0]
    piece_len = cot.shape[1]
    chunk = width // CHUNKS
    blocks = piece_len // BLOCK
    cols = piece_len // shards
    in_feats = feats.shape[1]
    halves = in_feats // BLOCK
    parts = (width // ROWS) * halves

    def copy(src, dst, ss, rs, **where):
        where = {"node": node, "rep": rep, "feat": feat, **where}
        return pltpu.make_async_remote_copy(
            src_ref=src, dst_ref=dst, send_sem=ss, recv_sem=rs, device_id=where, device_id_type=MESH
        )

    def flip(index, mask):
        bit = 1
        while bit <= mask:
            if mask & bit:
                index = index + bit * (1 - 2 * lax.rem(index // bit, 2))
            bit *= 2
        return index

    powers = all(n & (n - 1) == 0 for n in (groups, pieces, shards))
    flips = sorted(
        ((z, n, r) for z in range(shards) for n in range(groups) for r in range(pieces) if z or n or r),
        key=lambda f: (-f[0], -(f[1] > 0) - (f[2] > 1)))

    def peer_of(off):
        peer = lax.rem(me + off, devices)
        return {
            "node": peer // (pieces * shards),
            "rep": lax.rem(peer // shards, pieces),
            "feat": lax.rem(peer, shards),
        }

    barrier = pltpu.get_barrier_semaphore()

    def greet(**where):
        where = {"node": node, "rep": rep, "feat": feat, **where}
        pl.semaphore_signal(barrier, inc=1, device_id=where, device_id_type=MESH)

    for off in range(1, groups):
        greet(node=lax.rem(node + off, groups))
    for off in range(1, pieces):
        greet(rep=lax.rem(rep + off, pieces))
    pl.when(feat < shards - 1)(lambda: greet(feat=feat + 1))
    pl.when(feat > 0)(lambda: greet(feat=feat - 1))

    loads = [
        pltpu.make_async_copy(cot_hbm, cot, load_sem.at[0]),
        pltpu.make_async_copy(pre_hbm, pre, load_sem.at[1]),
        pltpu.make_async_copy(feat_hbm, feats.at[feat], load_sem.at[2]),
        pltpu.make_async_copy(tiles_hbm, tiles, load_sem.at[3]),
        pltpu.make_async_copy(source_hbm, source_ref, load_sem.at[4]),
        pltpu.make_async_copy(target_hbm, target_ref, load_sem.at[5]),
        pltpu.make_async_copy(count_hbm, count_ref, load_sem.at[6]),
    ]
    for load in loads:
        load.start()
    ends = jnp.where(feat == 0, 1, 0) + jnp.where(feat == shards - 1, 1, 0)
    pl.semaphore_wait(barrier, groups + pieces - ends)

    sends = []
    def relay(step, sub, block, to):
        rows = pl.ds(sub * (in_feats // SUBS), in_feats // SUBS)
        way = 0 if to > 0 else 1
        part = feats.at[block, rows]
        return copy(feat_hbm.at[rows] if step == 0 else part, part, f_ss.at[way, step, sub], f_rs.at[way, step, sub], feat=feat + to)

    def outgoing(step, sub, act):
        for to, ok in ((1, feat < shards - 1), (-1, feat > 0)):
            block = feat - to * step

            @pl.when(ok & (block >= 0) & (block < shards))
            def _():
                act(relay(step, sub, block, to))

    def pass_on(step, sub):
        outgoing(step, sub, lambda c: c.start())

    def settle(step, sub):
        outgoing(step, sub, lambda c: c.wait_send())

    def arrive(step, sub):
        for to in (1, -1):
            block = feat - to * (step + 1)

            @pl.when((block >= 0) & (block < shards))
            def _():
                relay(step, sub, block, to).wait_recv()

    todo = [(step, sub) for step in range(shards - 1) for sub in range(SUBS)]

    def forward(count):
        for step, sub in todo[:count]:
            arrive(step, sub)
            if step < shards - 2:
                pass_on(step + 1, sub)
        del todo[:count]

    for sub in range(SUBS):
        pass_on(0, sub)

    loads[0].wait()
    loads[1].wait()
    for h in range(CHUNKS):
        rows = pl.ds(h * chunk, chunk)
        for d in range(blocks):
            c = cot[rows, pl.ds(d * BLOCK, BLOCK)]
            own_grad[h, d] = jnp.where(pre[rows, pl.ds(d * BLOCK, BLOCK)] > 0, c, jnp.zeros_like(c))
    for h in range(CHUNKS):
        for off in range(1, groups):
            sends.append(copy(
                own_grad.at[h], grads[h].at[off - 1], x_ss.at[h, off], x_rs.at[h, off],
                node=lax.rem(node + off, groups)))
            sends[-1].start()

    for load in loads[3:]:
        load.wait()
    for g in range(groups):
        s = lax.rem(node - g + groups, groups)
        for t in range(slots):
            count = jnp.full((1, BLOCK), count_ref[s], jnp.int32)
            target = jnp.full((1, BLOCK), target_ref[0, s, 0, t], jnp.int32)
            tgt[0, pl.ds(g * slots + t, 1), :] = jnp.where(count > t, target, jnp.full_like(target, -1))
    for t in range(slots):
        block = source_ref[0, node, 0, t]
        picked = jnp.concatenate([own_grad[h, block] for h in range(CHUNKS)], axis=0)
        out = jnp.dot(picked, tiles[0, node, 0, t], preferred_element_type=jnp.float32)
        for h in range(CHUNKS):
            part = out[h * chunk:(h + 1) * chunk]
            own_prod[h, t] = part
            prod_a[0, h, t] = part.astype(jnp.bfloat16)
    for off in range(1, pieces):
        to = lax.rem(rep + off, pieces)
        sends.append(copy(tgt.at[0], tgt.at[off], t_ss.at[off], t_rs.at[off], rep=to))
        sends[-1].start()
        sends.append(copy(prod_a.at[0], prod_a.at[off], a_ss.at[off], a_rs.at[off], rep=to))
        sends[-1].start()

    def other_products(h, off):
        s = lax.rem(node - off + groups, groups)
        for t in range(slots):
            out = jnp.dot(grads[h][off - 1, source_ref[0, s, 0, t]], tiles[0, s, 0, t],
                          preferred_element_type=jnp.float32)
            own_prod[h, off * slots + t] = out
            prod_b[0, h, (off - 1) * slots + t] = out.astype(jnp.bfloat16)

    for h in range(CHUNKS):
        for off in range(1, groups):
            copy(own_grad.at[h], grads[h].at[off - 1], x_ss.at[h, off], x_rs.at[h, off]).wait_recv()
        if groups <= 4:
            for off in range(1, groups):
                other_products(h, off)
        else:
            lax.fori_loop(1, groups, lambda off, carry, h=h: (other_products(h, off), carry)[1], 0)
        for off in range(1, pieces):
            sends.append(copy(
                prod_b.at[0, h], prod_b.at[off, h], b_ss.at[h, off], b_rs.at[h, off],
                rep=lax.rem(rep + off, pieces)))
            sends[-1].start()
        forward(SUBS // CHUNKS)

    def add_up(total, from_rep, first, count, read):
        def step(n, total):
            value = read(n).astype(jnp.float32)
            to = tgt[from_rep, pl.ds(first + n, 1), :]
            zero = jnp.zeros_like(value)
            return tuple(
                part + jnp.where(jnp.broadcast_to(to == rep * blocks + d, value.shape), value, zero)
                for d, part in enumerate(total)
            )

        return lax.fori_loop(0, count, step, total, unroll=count <= 8)

    def add_near(h):
        total = tuple(jnp.zeros((chunk, BLOCK), jnp.float32) for _ in range(blocks))
        total = add_up(total, 0, 0, groups * slots, lambda n: own_prod[h, n])
        for off in range(1, pieces):
            total = add_up(total, off, 0, slots, lambda n, off=off: prod_a[off, h, n])
        for d in range(blocks):
            acc[h, d] = total[d]

    for off in range(1, pieces):
        copy(tgt.at[0], tgt.at[off], t_ss.at[off], t_rs.at[off]).wait_recv()
        copy(prod_a.at[0], prod_a.at[off], a_ss.at[off], a_rs.at[off]).wait_recv()
    for h in range(CHUNKS):
        add_near(h)

    per = cols // BLOCK
    for h in range(CHUNKS):
        forward(SUBS // CHUNKS)
        for off in range(1, pieces):
            copy(prod_b.at[0, h], prod_b.at[off, h], b_ss.at[h, off], b_rs.at[h, off]).wait_recv()
        total = tuple(acc[h, d] for d in range(blocks))
        for off in range(1, pieces):
            total = add_up(
                total, off, slots, (groups - 1) * slots, lambda n, h=h, off=off: prod_b[off, h, n])
        for d in range(blocks):
            aggs[d // per, pl.ds(h * chunk, chunk), pl.ds((d % per) * BLOCK, BLOCK)] = total[d].astype(jnp.bfloat16)
    agg_all[feat] = aggs[feat]

    forward(len(todo))
    loads[2].wait()
    scale = 1.0 / math.sqrt(piece_len * plane)
    wt = jnp.zeros((width, in_feats), jnp.float32)
    for z in range(shards):
        wt += lax.dot_general(
            aggs[z], feats[z], (((1,), (1,)), ((), ())), preferred_element_type=jnp.float32)
    wt *= scale
    for p in range(parts):
        part = wt[(p // halves) * ROWS:(p // halves + 1) * ROWS, (p % halves) * BLOCK:(p % halves + 1) * BLOCK]
        wt_own[p] = part
        rs_send[p] = part.astype(jnp.bfloat16)

    place = node * pieces + rep

    def to_reducer(q):
        return copy(
            rs_send.at[q], rs_recv.at[lax.rem(place - q + plane, plane)], r_ss.at[q], r_rs,
            node=q // pieces, rep=lax.rem(q, pieces))

    if plane == parts:
        for off in range(1, plane):
            sends.append(to_reducer(lax.rem(place + off, plane)))
            sends[-1].start()
    else:
        for q in range(parts):
            @pl.when(place != q)
            def _():
                to_reducer(q).start()

    for off in range(1, shards):
        to = lax.rem(feat + off, shards)
        sends.append(copy(aggs.at[to], agg_all.at[feat], z_ss.at[off], z_rs.at[off], feat=to))
        sends[-1].start()

    def reduce_and_send():
        pltpu.make_async_copy(
            rs_recv.at[pl.ds(1, plane - 1)], rs_recv.at[pl.ds(1, plane - 1)], r_rs).wait()
        total = lax.fori_loop(
            1, plane, lambda j, value: value + rs_recv[j].astype(jnp.float32), wt_own[place],
            unroll=plane <= 8)
        ag_send[...] = total.astype(jnp.bfloat16)
        mine = feat * parts + place
        gathered[mine] = ag_send[...]

        if powers and devices <= MAX_SENDS:
            for off, (z, n, r) in enumerate(flips, 1):
                copy(ag_send, gathered.at[mine], g_ss.at[off], g_rs,
                     node=flip(node, n), rep=flip(rep, r), feat=flip(feat, z)).start()
            return

        def send(off, carry):
            if devices - 1 > MAX_SENDS:
                @pl.when(off > MAX_SENDS)
                def _():
                    copy(ag_send, gathered.at[mine], g_ss.at[lax.rem(off, MAX_SENDS)], g_rs).wait_send()
            copy(ag_send, gathered.at[mine], g_ss.at[lax.rem(off, MAX_SENDS)], g_rs,
                 **peer_of(off)).start()
            return carry

        lax.fori_loop(1, devices, send, 0)

    if plane == parts:
        reduce_and_send()
    else:
        pl.when(place < parts)(reduce_and_send)

    for off in range(1, shards):
        origin = lax.rem(feat - off + shards, shards)
        copy(aggs.at[0], agg_all.at[origin], z_ss.at[off], z_rs.at[off]).wait_recv()

    stacked_ref[...] = agg_all[...].reshape(shards * width, cols)

    def all_but(k):
        pltpu.make_async_copy(gathered.at[pl.ds(0, shards * parts - k)],
                              gathered.at[pl.ds(0, shards * parts - k)], g_rs).wait()

    if plane == parts:
        all_but(1)
    else:
        pl.when(place < parts)(lambda: all_but(1))
        pl.when(place >= parts)(lambda: all_but(0))
    all_ref[...] = gathered[...]

    def drain():
        def wait(off, carry):
            copy(ag_send, gathered.at[0], g_ss.at[lax.rem(off, MAX_SENDS)], g_rs).wait_send()
            return carry

        lax.fori_loop(max(1, devices - MAX_SENDS), devices, wait, 0)

    if plane == parts:
        drain()
    else:
        pl.when(place < parts)(drain)
        for q in range(parts):
            @pl.when(place != q)
            def _():
                to_reducer(q).wait_send()
    for step in range(shards - 1):
        for sub in range(SUBS):
            settle(step, sub)
    for sent in sends:
        sent.wait_send()


def finish(halves, weight_ref, stacked_ref, all_ref, ig_ref, wg_ref):
    ig_ref[...] = jnp.dot(
        weight_ref[...], stacked_ref[...], preferred_element_type=jnp.float32).astype(jnp.bfloat16)
    bands = all_ref.shape[0] // halves
    for half in range(halves):
        side = jnp.concatenate([all_ref[b * halves + half] for b in range(bands)], axis=0)
        wg_ref[pl.ds(half * BLOCK, BLOCK), :] = side.astype(jnp.float32).T


def shards_step(groups, pieces, shards, cotangent, preact, features, weight, tile_values,
                source_blocks, target_blocks, tile_counts):
    width, piece_len = cotangent.shape
    slots = tile_values.shape[3]
    chunk = width // CHUNKS
    blocks = piece_len // BLOCK
    cols = piece_len // shards
    in_feats = features.shape[0]
    plane = groups * pieces
    parts = (width // ROWS) * (in_feats // BLOCK)
    bf16, f32 = jnp.bfloat16, jnp.float32
    dma = pltpu.SemaphoreType.DMA
    hbm = pl.BlockSpec(memory_space=pl.ANY)
    vmem = pl.BlockSpec(memory_space=pltpu.VMEM)
    stacked, everything = pl.pallas_call(
        functools.partial(kernel, groups, pieces, shards),
        out_shape=(
            pltpu.VMEM((width * shards, cols), bf16),
            pltpu.VMEM((shards * parts, ROWS, BLOCK), bf16),
        ),
        in_specs=[hbm] * 7,
        out_specs=(vmem, vmem),
        scratch_shapes=[
            pltpu.VMEM((width, piece_len), bf16),
            pltpu.VMEM((width, piece_len), bf16),
            pltpu.VMEM(tile_values.shape, bf16),
            pltpu.VMEM((CHUNKS, blocks, chunk, BLOCK), bf16),
            [pltpu.VMEM((max(groups - 1, 1), blocks, chunk, BLOCK), bf16) for _ in range(CHUNKS)],
            pltpu.VMEM((shards, in_feats, cols), bf16),
            pltpu.VMEM((pieces, groups * slots, BLOCK), jnp.int32),
            pltpu.VMEM((CHUNKS, groups * slots, chunk, BLOCK), f32),
            pltpu.VMEM((pieces, CHUNKS, slots, chunk, BLOCK), bf16),
            pltpu.VMEM((pieces, CHUNKS, (groups - 1) * slots, chunk, BLOCK), bf16),
            pltpu.VMEM((CHUNKS, blocks, chunk, BLOCK), f32),
            pltpu.VMEM((shards, width, cols), bf16),
            pltpu.VMEM((shards, width, cols), bf16),
            pltpu.VMEM((parts, ROWS, BLOCK), f32),
            pltpu.VMEM((parts, ROWS, BLOCK), bf16),
            pltpu.VMEM((plane, ROWS, BLOCK), bf16),
            pltpu.VMEM((ROWS, BLOCK), bf16),
            pltpu.VMEM((shards * parts, ROWS, BLOCK), bf16),
            pltpu.SMEM(source_blocks.shape, jnp.int32),
            pltpu.SMEM(target_blocks.shape, jnp.int32),
            pltpu.SMEM((groups,), jnp.int32),
            dma((7,)),
            dma((CHUNKS, groups)), dma((CHUNKS, groups)),
            dma((2, shards, SUBS)), dma((2, shards, SUBS)),
            dma((pieces,)), dma((pieces,)),
            dma((pieces,)), dma((pieces,)),
            dma((CHUNKS, pieces)), dma((CHUNKS, pieces)),
            dma((shards,)), dma((shards,)),
            dma((parts,)), dma(()),
            dma((MAX_SENDS,)), dma(()),
        ],
        compiler_params=pltpu.CompilerParams(collective_id=0, has_side_effects=True, vmem_limit_bytes=40 * 2**20),
        name="graph_backward",
    )(*(pltpu.with_memory_space_constraint(a, pltpu.HBM) for a in (
        cotangent, preact, features, tile_values, source_blocks, target_blocks, tile_counts.reshape(groups))))
    return pl.pallas_call(
        functools.partial(finish, in_feats // BLOCK),
        out_shape=(
            jax.ShapeDtypeStruct((weight.shape[0], cols), bf16),
            jax.ShapeDtypeStruct((in_feats, width * shards), f32),
        ),
        in_specs=[vmem] * 3,
        out_specs=(vmem, vmem),
        name="finish",
        compiler_params=pltpu.CompilerParams(vmem_limit_bytes=16 * 2**20),
    )(weight, pltpu.with_memory_space_constraint(stacked, pltpu.VMEM), pltpu.with_memory_space_constraint(everything, pltpu.VMEM))


def solution(mesh):
    step = functools.partial(shards_step, mesh.shape["node"], mesh.shape["rep"], mesh.shape["feat"])
    in_specs = (
        P("feat", ("node", "rep")),
        P("feat", ("node", "rep")),
        P(None, ("node", "rep", "feat")),
        P(),
        P("node", None, "rep", None, None, None),
        P("node", None, "rep", None),
        P("node", None, "rep", None),
        P("node", None, "rep"),
    )
    out_specs = (P(None, ("node", "rep", "feat")), P())
    return jax.shard_map(step, mesh=mesh, in_specs=in_specs, out_specs=out_specs, check_vma=False)
```

```python
import functools
import math

import jax
import jax.numpy as jnp
from jax import lax
from jax.experimental import pallas as pl
from jax.experimental.pallas import tpu as pltpu
from jax.sharding import PartitionSpec as P

MESH = pl.DeviceIdType.MESH
BLOCK = 128
CHUNKS = 4
ROWS = 16
SUBS = 4
LAG = 1
AHEAD = (3, 2, 2, 2)
LATER = 3
NEAR = (2, 1, 1)
MAX_SENDS = 32


def kernel(
    groups, pieces, shards,
    cot_hbm, pre_hbm, feat_hbm, tiles_hbm, source_hbm, target_hbm, count_hbm,
    stacked_ref, all_ref,
    given, tiles, own_grad, grads, feats, tgt, own_prod, prod_a, prod_b, acc, aggs, agg_all,
    wt_own, rs_send, rs_recv, sent, gathered, lists, count_ref,
    load_sem, x_ss, x_rs, f_ss, f_rs, far_rs, t_ss, t_rs, a_ss, a_rs, b_ss, b_rs, z_ss, z_rs, r_ss, r_rs, g_ss, g_rs,
):
    node = lax.axis_index("node")
    rep = lax.axis_index("rep")
    feat = lax.axis_index("feat")
    devices = groups * pieces * shards
    plane = groups * pieces
    me = (node * pieces + rep) * shards + feat
    slots = tiles_hbm.shape[3]
    width, piece_len = given.shape[1:]
    chunk = width // CHUNKS
    blocks = piece_len // BLOCK
    cols = piece_len // shards
    in_feats = feats.shape[1]
    halves = in_feats // BLOCK
    parts = (width // ROWS) * halves

    def copy(src, dst, ss, rs, **where):
        where = {"node": node, "rep": rep, "feat": feat, **where}
        return pltpu.make_async_remote_copy(
            src_ref=src, dst_ref=dst, send_sem=ss, recv_sem=rs, device_id=where, device_id_type=MESH
        )

    def flip(index, mask):
        bit = 1
        while bit <= mask:
            if mask & bit:
                index = index + bit * (1 - 2 * lax.rem(index // bit, 2))
            bit *= 2
        return index

    powers = all(n & (n - 1) == 0 for n in (groups, pieces, shards))
    flips = sorted(
        ((z, n, r) for z in range(shards) for n in range(groups) for r in range(pieces) if z or n or r),
        key=lambda f: (-f[0], -(f[1] > 0) - (f[2] > 1)))

    def peer_of(off):
        peer = lax.rem(me + off, devices)
        return {
            "node": peer // (pieces * shards),
            "rep": lax.rem(peer // shards, pieces),
            "feat": lax.rem(peer, shards),
        }

    def everything(ref, sem):
        pltpu.make_async_copy(ref, ref, sem).wait()

    barrier = pltpu.get_barrier_semaphore()

    def greet(**where):
        where = {"node": node, "rep": rep, "feat": feat, **where}
        pl.semaphore_signal(barrier, inc=1, device_id=where, device_id_type=MESH)

    for off in range(1, groups):
        greet(node=lax.rem(node + off, groups))
    for off in range(1, pieces):
        greet(rep=lax.rem(rep + off, pieces))
    met = groups + pieces - 2
    for to in (1, -1):
        pl.when((feat + to >= 0) & (feat + to < shards))(lambda to=to: greet(feat=feat + to))
        met += jnp.where((feat + to >= 0) & (feat + to < shards), 1, 0)

    loads = [
        pltpu.make_async_copy(cot_hbm, given.at[0], load_sem.at[0]),
        pltpu.make_async_copy(pre_hbm, given.at[1], load_sem.at[0]),
        pltpu.make_async_copy(feat_hbm, feats.at[feat], load_sem.at[1]),
        pltpu.make_async_copy(tiles_hbm, tiles, load_sem.at[2]),
        pltpu.make_async_copy(source_hbm, lists.at[0], load_sem.at[3]),
        pltpu.make_async_copy(target_hbm, lists.at[1], load_sem.at[3]),
        pltpu.make_async_copy(count_hbm, count_ref, load_sem.at[4]),
    ]
    for load in loads:
        load.start()
    pl.semaphore_wait(barrier, met)

    def relay(hop, sub, block, way, to):
        rows = pl.ds(sub * (in_feats // SUBS), in_feats // SUBS)
        part = feats.at[block, rows]
        got = f_rs.at[way, hop - 1, sub] if hop < shards - 1 else far_rs.at[way]
        return copy(feat_hbm.at[rows] if hop == 1 else part, part, f_ss.at[way, hop - 1], got, feat=to)

    def inside(z):
        return (z >= 0) & (z < shards)

    def pass_on(hop, sub, way):
        to = 1 - 2 * way
        pl.when(inside(feat - to * (hop - 1)) & inside(feat + to))(
            lambda: relay(hop, sub, feat - to * (hop - 1), way, feat + to).start())

    def forward(*events):
        for way, hop, sub in events:
            to = 1 - 2 * way

            @pl.when(inside(feat - to * hop))
            def _():
                relay(hop, sub, feat - to * hop, way, feat).wait_recv()
            pass_on(hop + 1, sub, way)

    hops = range(1, shards)
    queue = sorted(
        ((hop - 1) * SUBS + sub + LAG * way, way, hop, sub) for way in (0, 1) for hop in hops[:-1] for sub in range(SUBS))
    queue = [event[1:] for event in queue]

    def step_on(count):
        forward(*queue[:count])
        del queue[:count]

    for sub in range(SUBS):
        for way in (0, 1):
            pass_on(1, sub, way)

    everything(given, load_sem.at[0])
    for h in range(CHUNKS):
        rows = pl.ds(h * chunk, chunk)
        for d in range(blocks):
            c = given[0, rows, pl.ds(d * BLOCK, BLOCK)]
            own_grad[h, d] = jnp.where(given[1, rows, pl.ds(d * BLOCK, BLOCK)] > 0, c, jnp.zeros_like(c))
    for h in range(CHUNKS):
        for off in range(1, groups):
            copy(own_grad.at[h], grads[h].at[off - 1], x_ss.at[h], x_rs.at[h],
                 node=lax.rem(node + off, groups)).start()

    loads[3].wait()
    everything(lists, load_sem.at[3])
    loads[6].wait()
    for g in range(groups):
        s = lax.rem(node - g + groups, groups)
        for t in range(slots):
            count = jnp.full((1, BLOCK), count_ref[s], jnp.int32)
            target = jnp.full((1, BLOCK), lists[1, 0, s, 0, t], jnp.int32)
            tgt[0, pl.ds(g * slots + t, 1), :] = jnp.where(count > t, target, jnp.full_like(target, -1))
    for t in range(slots):
        block = lists[0, 0, node, 0, t]
        picked = jnp.concatenate([own_grad[h, block] for h in range(CHUNKS)], axis=0)
        out = jnp.dot(picked, tiles[0, node, 0, t], preferred_element_type=jnp.float32)
        for h in range(CHUNKS):
            part = out[h * chunk:(h + 1) * chunk]
            own_prod[h, t] = part
            prod_a[0, h, t] = part.astype(jnp.bfloat16)
    for off in range(1, pieces):
        to = lax.rem(rep + off, pieces)
        copy(tgt.at[0], tgt.at[off], t_ss, t_rs, rep=to).start()
        copy(prod_a.at[0], prod_a.at[off], a_ss, a_rs, rep=to).start()

    def other_products(h, off):
        s = lax.rem(node - off + groups, groups)
        for t in range(slots):
            out = jnp.dot(grads[h][off - 1, lists[0, 0, s, 0, t]], tiles[0, s, 0, t],
                          preferred_element_type=jnp.float32)
            own_prod[h, off * slots + t] = out
            prod_b[h, 0, (off - 1) * slots + t] = out.astype(jnp.bfloat16)

    for h in range(CHUNKS):
        step_on(AHEAD[h])
        everything(grads[h], x_rs.at[h])
        if groups <= 4:
            for off in range(1, groups):
                other_products(h, off)
        else:
            lax.fori_loop(1, groups, lambda off, carry, h=h: (other_products(h, off), carry)[1], 0)
        for off in range(1, pieces):
            copy(prod_b.at[h, 0], prod_b.at[h, off], b_ss, b_rs.at[h], rep=lax.rem(rep + off, pieces)).start()

    def add_up(total, from_rep, first, count, read):
        def step(n, total):
            value = read(n).astype(jnp.float32)
            to = tgt[from_rep, pl.ds(first + n, 1), :]
            zero = jnp.zeros_like(value)
            return tuple(
                part + jnp.where(jnp.broadcast_to(to == rep * blocks + d, value.shape), value, zero)
                for d, part in enumerate(total)
            )

        return lax.fori_loop(0, count, step, total, unroll=count <= 8)

    def add_near(h):
        total = tuple(jnp.zeros((chunk, BLOCK), jnp.float32) for _ in range(blocks))
        total = add_up(total, 0, 0, groups * slots, lambda n: own_prod[h, n])
        for off in range(1, pieces):
            total = add_up(total, off, 0, slots, lambda n, off=off: prod_a[off, h, n])
        for d in range(blocks):
            acc[h, d] = total[d]

    step_on(LATER)
    others = pl.ds(1, pieces - 1)
    everything(tgt.at[others], t_rs)
    everything(prod_a.at[others], a_rs)
    for h in range(CHUNKS):
        step_on(NEAR[h] if h < len(NEAR) else 0)
        add_near(h)

    per = cols // BLOCK
    for h in range(CHUNKS):
        everything(prod_b.at[h, pl.ds(1, pieces - 1)], b_rs.at[h])
        total = tuple(acc[h, d] for d in range(blocks))
        for off in range(1, pieces):
            total = add_up(
                total, off, slots, (groups - 1) * slots, lambda n, h=h, off=off: prod_b[h, off, n])
        for d in range(blocks):
            aggs[d // per, pl.ds(h * chunk, chunk), pl.ds((d % per) * BLOCK, BLOCK)] = total[d].astype(jnp.bfloat16)
    agg_all[feat] = aggs[feat]

    step_on(len(queue))
    for way in (0, 1):
        pl.when(inside(feat - (1 - 2 * way) * (shards - 1)))(
            lambda way=way: everything(feats.at[feat - (1 - 2 * way) * (shards - 1)], far_rs.at[way]))
    loads[2].wait()
    scale = 1.0 / math.sqrt(piece_len * plane)
    wt = jnp.zeros((width, in_feats), jnp.float32)
    for z in range(shards):
        wt += lax.dot_general(
            aggs[z], feats[z], (((1,), (1,)), ((), ())), preferred_element_type=jnp.float32)
    wt *= scale
    for p in range(parts):
        part = wt[(p // halves) * ROWS:(p // halves + 1) * ROWS, (p % halves) * BLOCK:(p % halves + 1) * BLOCK]
        wt_own[p] = part
        rs_send[p] = part.astype(jnp.bfloat16)

    place = node * pieces + rep

    def to_reducer(q):
        return copy(
            rs_send.at[q], rs_recv.at[lax.rem(place - q + plane, plane)], r_ss, r_rs,
            node=q // pieces, rep=lax.rem(q, pieces))

    if plane == parts:
        for off in range(1, plane):
            to_reducer(lax.rem(place + off, plane)).start()
    else:
        for q in range(parts):
            @pl.when(place != q)
            def _():
                to_reducer(q).start()

    for off in range(1, shards):
        to = lax.rem(feat + off, shards)
        copy(aggs.at[to], agg_all.at[feat], z_ss, z_rs, feat=to).start()

    def reduce_and_send():
        pltpu.make_async_copy(
            rs_recv.at[pl.ds(1, plane - 1)], rs_recv.at[pl.ds(1, plane - 1)], r_rs).wait()
        total = lax.fori_loop(
            1, plane, lambda j, value: value + rs_recv[j].astype(jnp.float32), wt_own[place],
            unroll=plane <= 8)
        mine = feat * parts + place
        gathered[mine] = total.astype(jnp.bfloat16)

        if powers and devices <= MAX_SENDS:
            for z, n, r in flips:
                copy(gathered.at[mine], gathered.at[mine], g_ss, g_rs,
                     node=flip(node, n), rep=flip(rep, r), feat=flip(feat, z)).start()
            return

        def send(off, carry):
            copy(gathered.at[mine], gathered.at[mine], g_ss, g_rs, **peer_of(off)).start()
            return carry

        lax.fori_loop(1, devices, send, 0)

    if plane == parts:
        reduce_and_send()
    else:
        pl.when(place < parts)(reduce_and_send)

    everything(agg_all.at[pl.ds(0, shards - 1)], z_rs)

    stacked_ref[...] = agg_all[...].reshape(shards * width, cols)

    for way in (0, 1):
        to = 1 - 2 * way
        for hop in hops:
            pl.when(inside(feat - to * (hop - 1)) & inside(feat + to))(
                lambda way=way, hop=hop: everything(feats.at[0], f_ss.at[way, hop - 1]))
    for h in range(CHUNKS):
        everything(grads[h], x_ss.at[h])
    everything(tgt.at[others], t_ss)
    everything(prod_a.at[others], a_ss)
    everything(prod_b.at[:, others], b_ss)
    everything(agg_all.at[pl.ds(0, shards - 1)], z_ss)

    def reduced(count):
        everything(rs_send.at[pl.ds(0, count)], r_ss)

    if plane == parts:
        reduced(parts - 1)
    else:
        pl.when(place < parts)(lambda: reduced(parts - 1))
        pl.when(place >= parts)(lambda: reduced(parts))

    def all_but(k):
        pltpu.make_async_copy(gathered.at[pl.ds(0, shards * parts - k)],
                              gathered.at[pl.ds(0, shards * parts - k)], g_rs).wait()

    if plane == parts:
        all_but(1)
    else:
        pl.when(place < parts)(lambda: all_but(1))
        pl.when(place >= parts)(lambda: all_but(0))
    all_ref[...] = gathered[...]

    def drain():
        everything(sent, g_ss)

    if plane == parts:
        drain()
    else:
        pl.when(place < parts)(drain)


def finish(halves, weight_ref, stacked_ref, all_ref, ig_ref, wg_ref):
    ig_ref[...] = jnp.dot(
        weight_ref[...], stacked_ref[...], preferred_element_type=jnp.float32).astype(jnp.bfloat16)
    bands = all_ref.shape[0] // halves
    for half in range(halves):
        side = jnp.concatenate([all_ref[b * halves + half] for b in range(bands)], axis=0)
        wg_ref[pl.ds(half * BLOCK, BLOCK), :] = side.astype(jnp.float32).T


def shards_step(groups, pieces, shards, cotangent, preact, features, weight, tile_values,
                source_blocks, target_blocks, tile_counts):
    width, piece_len = cotangent.shape
    slots = tile_values.shape[3]
    chunk = width // CHUNKS
    blocks = piece_len // BLOCK
    cols = piece_len // shards
    in_feats = features.shape[0]
    plane = groups * pieces
    parts = (width // ROWS) * (in_feats // BLOCK)
    bf16, f32 = jnp.bfloat16, jnp.float32
    dma = pltpu.SemaphoreType.DMA
    hbm = pl.BlockSpec(memory_space=pl.ANY)
    vmem = pl.BlockSpec(memory_space=pltpu.VMEM)
    stacked, everything = pl.pallas_call(
        functools.partial(kernel, groups, pieces, shards),
        out_shape=(
            pltpu.VMEM((width * shards, cols), bf16),
            pltpu.VMEM((shards * parts, ROWS, BLOCK), bf16),
        ),
        in_specs=[hbm] * 7,
        out_specs=(vmem, vmem),
        scratch_shapes=[
            pltpu.VMEM((2, width, piece_len), bf16),
            pltpu.VMEM(tile_values.shape, bf16),
            pltpu.VMEM((CHUNKS, blocks, chunk, BLOCK), bf16),
            [pltpu.VMEM((groups - 1, blocks, chunk, BLOCK), bf16) for _ in range(CHUNKS)],
            pltpu.VMEM((shards, in_feats, cols), bf16),
            pltpu.VMEM((pieces, groups * slots, BLOCK), jnp.int32),
            pltpu.VMEM((CHUNKS, groups * slots, chunk, BLOCK), f32),
            pltpu.VMEM((pieces, CHUNKS, slots, chunk, BLOCK), bf16),
            pltpu.VMEM((CHUNKS, pieces, (groups - 1) * slots, chunk, BLOCK), bf16),
            pltpu.VMEM((CHUNKS, blocks, chunk, BLOCK), f32),
            pltpu.VMEM((shards, width, cols), bf16),
            pltpu.VMEM((shards, width, cols), bf16),
            pltpu.VMEM((parts, ROWS, BLOCK), f32),
            pltpu.VMEM((parts, ROWS, BLOCK), bf16),
            pltpu.VMEM((plane, ROWS, BLOCK), bf16),
            pltpu.VMEM((groups * pieces * shards - 1, ROWS, BLOCK), bf16),
            pltpu.VMEM((shards * parts, ROWS, BLOCK), bf16),
            pltpu.SMEM((2, *source_blocks.shape), jnp.int32),
            pltpu.SMEM((groups,), jnp.int32),
            dma((5,)),
            dma((CHUNKS,)), dma((CHUNKS,)),
            dma((2, shards - 1)), dma((2, max(shards - 2, 1), SUBS)), dma((2,)),
            dma(()), dma(()),
            dma(()), dma(()),
            dma(()), dma((CHUNKS,)),
            dma(()), dma(()),
            dma(()), dma(()),
            dma(()), dma(()),
        ],
        compiler_params=pltpu.CompilerParams(collective_id=0, has_side_effects=True, vmem_limit_bytes=40 * 2**20),
        name="graph_backward",
    )(*(pltpu.with_memory_space_constraint(a, pltpu.HBM) for a in (
        cotangent, preact, features, tile_values, source_blocks, target_blocks, tile_counts.reshape(groups))))
    return pl.pallas_call(
        functools.partial(finish, in_feats // BLOCK),
        out_shape=(
            jax.ShapeDtypeStruct((weight.shape[0], cols), bf16),
            jax.ShapeDtypeStruct((in_feats, width * shards), f32),
        ),
        in_specs=[vmem] * 3,
        out_specs=(vmem, vmem),
        name="finish",
        compiler_params=pltpu.CompilerParams(vmem_limit_bytes=16 * 2**20),
    )(weight, pltpu.with_memory_space_constraint(stacked, pltpu.VMEM), pltpu.with_memory_space_constraint(everything, pltpu.VMEM))


def solution(mesh):
    step = functools.partial(shards_step, mesh.shape["node"], mesh.shape["rep"], mesh.shape["feat"])
    in_specs = (
        P("feat", ("node", "rep")),
        P("feat", ("node", "rep")),
        P(None, ("node", "rep", "feat")),
        P(),
        P("node", None, "rep", None, None, None),
        P("node", None, "rep", None),
        P("node", None, "rep", None),
        P("node", None, "rep"),
    )
    out_specs = (P(None, ("node", "rep", "feat")), P())
    return jax.shard_map(step, mesh=mesh, in_specs=in_specs, out_specs=out_specs, check_vma=False)
```

```python
import functools
import math

import jax
import jax.numpy as jnp
from jax import lax
from jax.experimental import pallas as pl
from jax.experimental.pallas import tpu as pltpu
from jax.sharding import PartitionSpec as P

MESH = pl.DeviceIdType.MESH
BLOCK = 128
CHUNKS = 4
ROWS = 16
SUBS = 4
LAG = 0
AHEAD = (3, 2, 2, 2)
LATER = 3
NEAR = (2, 1, 1)
MAX_SENDS = 32


def kernel(
    groups, pieces, shards,
    cot_hbm, pre_hbm, feat_hbm, tiles_hbm, source_hbm, target_hbm, count_hbm,
    stacked_ref, all_ref,
    given, tiles, own_grad, grads, feats, tgt, own_prod, prod_a, prod_b, acc, aggs, agg_all,
    wt_own, rs_send, rs_recv, sent, bulk, gathered, lists, count_ref,
    load_sem, out_ss, x_rs, f_ss, f_rs, far_rs, t_rs, a_rs, b_rs, z_rs, r_ss, r_rs, g_ss, g_rs,
):
    node = lax.axis_index("node")
    rep = lax.axis_index("rep")
    feat = lax.axis_index("feat")
    devices = groups * pieces * shards
    plane = groups * pieces
    me = (node * pieces + rep) * shards + feat
    slots = tiles_hbm.shape[3]
    width, piece_len = given.shape[1:]
    chunk = width // CHUNKS
    blocks = piece_len // BLOCK
    cols = piece_len // shards
    in_feats = feats.shape[1]
    halves = in_feats // BLOCK
    parts = (width // ROWS) * halves

    def copy(src, dst, ss, rs, **where):
        where = {"node": node, "rep": rep, "feat": feat, **where}
        return pltpu.make_async_remote_copy(
            src_ref=src, dst_ref=dst, send_sem=ss, recv_sem=rs, device_id=where, device_id_type=MESH
        )

    def flip(index, mask):
        bit = 1
        while bit <= mask:
            if mask & bit:
                index = index + bit * (1 - 2 * lax.rem(index // bit, 2))
            bit *= 2
        return index

    powers = all(n & (n - 1) == 0 for n in (groups, pieces))
    flips = sorted(
        ((n, r) for n in range(groups) for r in range(pieces)), key=lambda f: -(f[0] > 0) - (f[1] > 1))

    def peer_of(off):
        peer = lax.rem(me + off, devices)
        return {
            "node": peer // (pieces * shards),
            "rep": lax.rem(peer // shards, pieces),
            "feat": lax.rem(peer, shards),
        }

    def everything(ref, sem):
        pltpu.make_async_copy(ref, ref, sem).wait()

    barrier = pltpu.get_barrier_semaphore()

    def greet(**where):
        where = {"node": node, "rep": rep, "feat": feat, **where}
        pl.semaphore_signal(barrier, inc=1, device_id=where, device_id_type=MESH)

    for off in range(1, groups):
        greet(node=lax.rem(node + off, groups))
    for off in range(1, pieces):
        greet(rep=lax.rem(rep + off, pieces))
    met = groups + pieces - 2
    for to in (1, -1):
        pl.when((feat + to >= 0) & (feat + to < shards))(lambda to=to: greet(feat=feat + to))
        met += jnp.where((feat + to >= 0) & (feat + to < shards), 1, 0)

    loads = [
        pltpu.make_async_copy(cot_hbm, given.at[0], load_sem.at[0]),
        pltpu.make_async_copy(pre_hbm, given.at[1], load_sem.at[0]),
        pltpu.make_async_copy(feat_hbm, feats.at[feat], load_sem.at[1]),
        pltpu.make_async_copy(tiles_hbm, tiles, load_sem.at[2]),
        pltpu.make_async_copy(source_hbm, lists.at[0], load_sem.at[3]),
        pltpu.make_async_copy(target_hbm, lists.at[1], load_sem.at[3]),
        pltpu.make_async_copy(count_hbm, count_ref, load_sem.at[4]),
    ]
    for load in loads:
        load.start()
    pl.semaphore_wait(barrier, met)

    def relay(hop, sub, block, way, to):
        rows = pl.ds(sub * (in_feats // SUBS), in_feats // SUBS)
        part = feats.at[block, rows]
        got = f_rs.at[way, hop - 1, sub] if hop < shards - 1 else far_rs.at[way]
        return copy(feat_hbm.at[rows] if hop == 1 else part, part, f_ss.at[way], got, feat=to)

    def inside(z):
        return (z >= 0) & (z < shards)

    def pass_on(hop, sub, way):
        to = 1 - 2 * way
        pl.when(inside(feat - to * (hop - 1)) & inside(feat + to))(
            lambda: relay(hop, sub, feat - to * (hop - 1), way, feat + to).start())

    def forward(*events):
        for way, hop, sub in events:
            to = 1 - 2 * way

            @pl.when(inside(feat - to * hop) & inside(feat + to))
            def _():
                relay(hop, sub, feat - to * hop, way, feat).wait_recv()
                relay(hop + 1, sub, feat - to * hop, way, feat + to).start()

    def settle(count):
        for way in (0, 1):
            to = 1 - 2 * way

            @pl.when(feat == (shards - 1) * (1 - way))
            def _():
                for hop in hops[:-1][-count:] if count else ():
                    for sub in range(SUBS):
                        relay(hop, sub, feat - to * hop, way, feat).wait_recv()
                if not count:
                    everything(feats.at[feat - to * (shards - 1)], far_rs.at[way])

    hops = range(1, shards)
    queue = sorted(
        ((hop - 1) * SUBS + sub + LAG * way, way, hop, sub) for way in (0, 1) for hop in hops[:-1] for sub in range(SUBS))
    queue = [event[1:] for event in queue]

    def step_on(count):
        forward(*queue[:count])
        del queue[:count]

    for sub in range(SUBS):
        for way in (0, 1):
            pass_on(1, sub, way)

    everything(given, load_sem.at[0])
    for h in range(CHUNKS):
        rows = pl.ds(h * chunk, chunk)
        for d in range(blocks):
            c = given[0, rows, pl.ds(d * BLOCK, BLOCK)]
            own_grad[h, d] = jnp.where(given[1, rows, pl.ds(d * BLOCK, BLOCK)] > 0, c, jnp.zeros_like(c))
    for h in range(CHUNKS):
        for off in range(1, groups):
            copy(own_grad.at[h], grads[h].at[off - 1], out_ss, x_rs.at[h],
                 node=lax.rem(node + off, groups)).start()

    loads[3].wait()
    everything(lists, load_sem.at[3])
    loads[6].wait()
    for g in range(groups):
        s = lax.rem(node - g + groups, groups)
        for t in range(slots):
            count = jnp.full((1, BLOCK), count_ref[s], jnp.int32)
            target = jnp.full((1, BLOCK), lists[1, 0, s, 0, t], jnp.int32)
            tgt[0, pl.ds(g * slots + t, 1), :] = jnp.where(count > t, target, jnp.full_like(target, -1))
    for t in range(slots):
        block = lists[0, 0, node, 0, t]
        picked = jnp.concatenate([own_grad[h, block] for h in range(CHUNKS)], axis=0)
        out = jnp.dot(picked, tiles[0, node, 0, t], preferred_element_type=jnp.float32)
        for h in range(CHUNKS):
            part = out[h * chunk:(h + 1) * chunk]
            own_prod[h, t] = part
            prod_a[0, h, t] = part.astype(jnp.bfloat16)
    for off in range(1, pieces):
        to = lax.rem(rep + off, pieces)
        copy(tgt.at[0], tgt.at[off], out_ss, t_rs, rep=to).start()
        copy(prod_a.at[0], prod_a.at[off], out_ss, a_rs, rep=to).start()

    def other_products(h, off):
        s = lax.rem(node - off + groups, groups)
        for t in range(slots):
            out = jnp.dot(grads[h][off - 1, lists[0, 0, s, 0, t]], tiles[0, s, 0, t],
                          preferred_element_type=jnp.float32)
            own_prod[h, off * slots + t] = out
            prod_b[h, 0, (off - 1) * slots + t] = out.astype(jnp.bfloat16)

    for h in range(CHUNKS):
        step_on(AHEAD[h])
        everything(grads[h], x_rs.at[h])
        if groups <= 4:
            for off in range(1, groups):
                other_products(h, off)
        else:
            lax.fori_loop(1, groups, lambda off, carry, h=h: (other_products(h, off), carry)[1], 0)
        for off in range(1, pieces):
            copy(prod_b.at[h, 0], prod_b.at[h, off], out_ss, b_rs.at[h], rep=lax.rem(rep + off, pieces)).start()

    def add_up(total, from_rep, first, count, read):
        def step(n, total):
            value = read(n).astype(jnp.float32)
            to = tgt[from_rep, pl.ds(first + n, 1), :]
            zero = jnp.zeros_like(value)
            return tuple(
                part + jnp.where(jnp.broadcast_to(to == rep * blocks + d, value.shape), value, zero)
                for d, part in enumerate(total)
            )

        return lax.fori_loop(0, count, step, total, unroll=count <= 8)

    def add_near(h):
        total = tuple(jnp.zeros((chunk, BLOCK), jnp.float32) for _ in range(blocks))
        total = add_up(total, 0, 0, groups * slots, lambda n: own_prod[h, n])
        for off in range(1, pieces):
            total = add_up(total, off, 0, slots, lambda n, off=off: prod_a[off, h, n])
        for d in range(blocks):
            acc[h, d] = total[d]

    step_on(LATER)
    others = pl.ds(1, pieces - 1)
    everything(tgt.at[others], t_rs)
    everything(prod_a.at[others], a_rs)
    for h in range(CHUNKS):
        step_on(NEAR[h] if h < len(NEAR) else 0)
        add_near(h)

    per = cols // BLOCK
    for h in range(CHUNKS):
        everything(prod_b.at[h, pl.ds(1, pieces - 1)], b_rs.at[h])
        total = tuple(acc[h, d] for d in range(blocks))
        for off in range(1, pieces):
            total = add_up(
                total, off, slots, (groups - 1) * slots, lambda n, h=h, off=off: prod_b[h, off, n])
        for d in range(blocks):
            aggs[d // per, pl.ds(h * chunk, chunk), pl.ds((d % per) * BLOCK, BLOCK)] = total[d].astype(jnp.bfloat16)
    agg_all[feat] = aggs[feat]

    step_on(len(queue))
    settle(shards - 2)
    loads[2].wait()
    scale = 1.0 / math.sqrt(piece_len * plane)
    wt = jnp.zeros((width, in_feats), jnp.float32)
    for k in range(shards):
        if k == shards - 1:
            settle(0)
        z = jnp.where(feat < shards // 2, k, shards - 1 - k)
        wt += lax.dot_general(
            aggs[z], feats[z], (((1,), (1,)), ((), ())), preferred_element_type=jnp.float32)
    wt *= scale
    for p in range(parts):
        part = wt[(p // halves) * ROWS:(p // halves + 1) * ROWS, (p % halves) * BLOCK:(p % halves + 1) * BLOCK]
        wt_own[p] = part
        rs_send[p] = part.astype(jnp.bfloat16)

    place = node * pieces + rep

    def to_reducer(q):
        return copy(
            rs_send.at[q], rs_recv.at[lax.rem(place - q + plane, plane)], r_ss, r_rs,
            node=q // pieces, rep=lax.rem(q, pieces))

    if plane == parts:
        for off in range(1, plane):
            to_reducer(lax.rem(place + off, plane)).start()
    else:
        for q in range(parts):
            @pl.when(place != q)
            def _():
                to_reducer(q).start()

    for off in range(1, shards):
        to = lax.rem(feat + off, shards)
        copy(aggs.at[to], agg_all.at[feat], out_ss, z_rs, feat=to).start()

    def reduce_and_send():
        pltpu.make_async_copy(
            rs_recv.at[pl.ds(1, plane - 1)], rs_recv.at[pl.ds(1, plane - 1)], r_rs).wait()
        total = lax.fori_loop(
            1, plane, lambda j, value: value + rs_recv[j].astype(jnp.float32), wt_own[place],
            unroll=plane <= 8)
        mine = feat * parts + place
        gathered[mine] = total.astype(jnp.bfloat16)

        if powers and devices <= MAX_SENDS:
            for z in range(shards):
                for n, r in flips:
                    def start(z=z, n=n, r=r):
                        copy(gathered.at[mine], gathered.at[mine], g_ss, g_rs,
                             node=flip(node, n), rep=flip(rep, r), feat=z).start()

                    if n or r:
                        start()
                    else:
                        pl.when(feat != z)(start)
            return

        def send(off, carry):
            copy(gathered.at[mine], gathered.at[mine], g_ss, g_rs, **peer_of(off)).start()
            return carry

        lax.fori_loop(1, devices, send, 0)

    if plane == parts:
        reduce_and_send()
    else:
        pl.when(place < parts)(reduce_and_send)

    everything(agg_all.at[pl.ds(0, shards - 1)], z_rs)

    stacked_ref[...] = agg_all[...].reshape(shards * width, cols)

    for count in hops:
        pl.when(feat == count - 1)(lambda count=count: everything(feats.at[pl.ds(0, count)], f_ss.at[0]))
        pl.when(feat == shards - count)(lambda count=count: everything(feats.at[pl.ds(0, count)], f_ss.at[1]))
    everything(bulk, out_ss)

    def reduced(count):
        everything(rs_send.at[pl.ds(0, count)], r_ss)

    if plane == parts:
        reduced(parts - 1)
    else:
        pl.when(place < parts)(lambda: reduced(parts - 1))
        pl.when(place >= parts)(lambda: reduced(parts))

    def all_but(k):
        pltpu.make_async_copy(gathered.at[pl.ds(0, shards * parts - k)],
                              gathered.at[pl.ds(0, shards * parts - k)], g_rs).wait()

    if plane == parts:
        all_but(1)
    else:
        pl.when(place < parts)(lambda: all_but(1))
        pl.when(place >= parts)(lambda: all_but(0))
    all_ref[...] = gathered[...]

    def drain():
        everything(sent, g_ss)

    if plane == parts:
        drain()
    else:
        pl.when(place < parts)(drain)


def finish(halves, weight_ref, stacked_ref, all_ref, ig_ref, wg_ref):
    ig_ref[...] = jnp.dot(
        weight_ref[...], stacked_ref[...], preferred_element_type=jnp.float32).astype(jnp.bfloat16)
    bands = all_ref.shape[0] // halves
    for half in range(halves):
        side = jnp.concatenate([all_ref[b * halves + half] for b in range(bands)], axis=0)
        wg_ref[pl.ds(half * BLOCK, BLOCK), :] = side.astype(jnp.float32).T


def shards_step(groups, pieces, shards, cotangent, preact, features, weight, tile_values,
                source_blocks, target_blocks, tile_counts):
    width, piece_len = cotangent.shape
    slots = tile_values.shape[3]
    chunk = width // CHUNKS
    blocks = piece_len // BLOCK
    cols = piece_len // shards
    in_feats = features.shape[0]
    per = cols // BLOCK
    plane = groups * pieces
    parts = (width // ROWS) * (in_feats // BLOCK)
    bf16, f32 = jnp.bfloat16, jnp.float32
    dma = pltpu.SemaphoreType.DMA
    out_rows = (groups - 1) * width * blocks + (pieces - 1) * groups * slots * (2 + width) + (shards - 1) * width * per
    hbm = pl.BlockSpec(memory_space=pl.ANY)
    vmem = pl.BlockSpec(memory_space=pltpu.VMEM)
    stacked, everything = pl.pallas_call(
        functools.partial(kernel, groups, pieces, shards),
        out_shape=(
            pltpu.VMEM((width * shards, cols), bf16),
            pltpu.VMEM((shards * parts, ROWS, BLOCK), bf16),
        ),
        in_specs=[hbm] * 7,
        out_specs=(vmem, vmem),
        scratch_shapes=[
            pltpu.VMEM((2, width, piece_len), bf16),
            pltpu.VMEM(tile_values.shape, bf16),
            pltpu.VMEM((CHUNKS, blocks, chunk, BLOCK), bf16),
            [pltpu.VMEM((groups - 1, blocks, chunk, BLOCK), bf16) for _ in range(CHUNKS)],
            pltpu.VMEM((shards, in_feats, cols), bf16),
            pltpu.VMEM((pieces, groups * slots, BLOCK), jnp.int32),
            pltpu.VMEM((CHUNKS, groups * slots, chunk, BLOCK), f32),
            pltpu.VMEM((pieces, CHUNKS, slots, chunk, BLOCK), bf16),
            pltpu.VMEM((CHUNKS, pieces, (groups - 1) * slots, chunk, BLOCK), bf16),
            pltpu.VMEM((CHUNKS, blocks, chunk, BLOCK), f32),
            pltpu.VMEM((shards, width, cols), bf16),
            pltpu.VMEM((shards, width, cols), bf16),
            pltpu.VMEM((parts, ROWS, BLOCK), f32),
            pltpu.VMEM((parts, ROWS, BLOCK), bf16),
            pltpu.VMEM((plane, ROWS, BLOCK), bf16),
            pltpu.VMEM((groups * pieces * shards - 1, ROWS, BLOCK), bf16),
            pltpu.VMEM((out_rows, BLOCK), bf16),
            pltpu.VMEM((shards * parts, ROWS, BLOCK), bf16),
            pltpu.SMEM((2, *source_blocks.shape), jnp.int32),
            pltpu.SMEM((groups,), jnp.int32),
            dma((5,)),
            dma(()), dma((CHUNKS,)),
            dma((2,)), dma((2, max(shards - 2, 1), SUBS)), dma((2,)),
            dma(()), dma(()), dma((CHUNKS,)), dma(()),
            dma(()), dma(()),
            dma(()), dma(()),
        ],
        compiler_params=pltpu.CompilerParams(collective_id=0, has_side_effects=True, vmem_limit_bytes=40 * 2**20),
        name="graph_backward",
    )(*(pltpu.with_memory_space_constraint(a, pltpu.HBM) for a in (
        cotangent, preact, features, tile_values, source_blocks, target_blocks, tile_counts.reshape(groups))))
    return pl.pallas_call(
        functools.partial(finish, in_feats // BLOCK),
        out_shape=(
            jax.ShapeDtypeStruct((weight.shape[0], cols), bf16),
            jax.ShapeDtypeStruct((in_feats, width * shards), f32),
        ),
        in_specs=[vmem] * 3,
        out_specs=(vmem, vmem),
        name="finish",
        compiler_params=pltpu.CompilerParams(vmem_limit_bytes=16 * 2**20),
    )(weight, pltpu.with_memory_space_constraint(stacked, pltpu.VMEM), pltpu.with_memory_space_constraint(everything, pltpu.VMEM))


def solution(mesh):
    step = functools.partial(shards_step, mesh.shape["node"], mesh.shape["rep"], mesh.shape["feat"])
    in_specs = (
        P("feat", ("node", "rep")),
        P("feat", ("node", "rep")),
        P(None, ("node", "rep", "feat")),
        P(),
        P("node", None, "rep", None, None, None),
        P("node", None, "rep", None),
        P("node", None, "rep", None),
        P("node", None, "rep"),
    )
    out_specs = (P(None, ("node", "rep", "feat")), P())
    return jax.shard_map(step, mesh=mesh, in_specs=in_specs, out_specs=out_specs, check_vma=False)
```

```python
import functools
import math

import jax
import jax.numpy as jnp
from jax import lax
from jax.experimental import pallas as pl
from jax.experimental.pallas import tpu as pltpu
from jax.sharding import PartitionSpec as P

MESH = pl.DeviceIdType.MESH
BLOCK = 128
CHUNKS = 4
ROWS = 16
SUBS = 4
LAG = 0
AHEAD = (3, 2, 2, 2)
LATER = 3
NEAR = (2, 1, 1)
MAX_SENDS = 32


def kernel(
    groups, pieces, shards,
    cot_hbm, pre_hbm, feat_hbm, tiles_hbm, source_hbm, target_hbm, count_hbm, weight_hbm,
    mixed_ref, all_ref,
    given, tiles, weight, own_grad, grads, feats, tgt, own_prod, prod_a, prod_b, acc, aggs, agg_all,
    wt_own, rs_send, rs_recv, sent, bulk, gathered, lists, count_ref,
    load_sem, out_ss, x_rs, f_ss, f_rs, far_rs, t_rs, a_rs, b_rs, z_rs, r_ss, r_rs, g_ss, g_rs,
):
    node = lax.axis_index("node")
    rep = lax.axis_index("rep")
    feat = lax.axis_index("feat")
    devices = groups * pieces * shards
    plane = groups * pieces
    me = (node * pieces + rep) * shards + feat
    slots = tiles_hbm.shape[3]
    width, piece_len = given.shape[1:]
    chunk = width // CHUNKS
    blocks = piece_len // BLOCK
    cols = piece_len // shards
    in_feats = feats.shape[1]
    halves = in_feats // BLOCK
    parts = (width // ROWS) * halves

    def copy(src, dst, ss, rs, **where):
        where = {"node": node, "rep": rep, "feat": feat, **where}
        return pltpu.make_async_remote_copy(
            src_ref=src, dst_ref=dst, send_sem=ss, recv_sem=rs, device_id=where, device_id_type=MESH
        )

    def flip(index, mask):
        bit = 1
        while bit <= mask:
            if mask & bit:
                index = index + bit * (1 - 2 * lax.rem(index // bit, 2))
            bit *= 2
        return index

    powers = all(n & (n - 1) == 0 for n in (groups, pieces))
    flips = sorted(
        ((n, r) for n in range(groups) for r in range(pieces)), key=lambda f: -(f[0] > 0) - (f[1] > 1))

    def peer_of(off):
        peer = lax.rem(me + off, devices)
        return {
            "node": peer // (pieces * shards),
            "rep": lax.rem(peer // shards, pieces),
            "feat": lax.rem(peer, shards),
        }

    def everything(ref, sem):
        pltpu.make_async_copy(ref, ref, sem).wait()

    barrier = pltpu.get_barrier_semaphore()

    def greet(**where):
        where = {"node": node, "rep": rep, "feat": feat, **where}
        pl.semaphore_signal(barrier, inc=1, device_id=where, device_id_type=MESH)

    for off in range(1, groups):
        greet(node=lax.rem(node + off, groups))
    for off in range(1, pieces):
        greet(rep=lax.rem(rep + off, pieces))
    met = groups + pieces - 2
    for to in (1, -1):
        pl.when((feat + to >= 0) & (feat + to < shards))(lambda to=to: greet(feat=feat + to))
        met += jnp.where((feat + to >= 0) & (feat + to < shards), 1, 0)

    loads = [
        pltpu.make_async_copy(cot_hbm, given.at[0], load_sem.at[0]),
        pltpu.make_async_copy(pre_hbm, given.at[1], load_sem.at[0]),
        pltpu.make_async_copy(feat_hbm, feats.at[feat], load_sem.at[1]),
        pltpu.make_async_copy(tiles_hbm, tiles, load_sem.at[2]),
        pltpu.make_async_copy(source_hbm, lists.at[0], load_sem.at[3]),
        pltpu.make_async_copy(target_hbm, lists.at[1], load_sem.at[3]),
        pltpu.make_async_copy(count_hbm, count_ref, load_sem.at[4]),
        pltpu.make_async_copy(weight_hbm, weight, load_sem.at[5]),
    ]
    for load in loads:
        load.start()
    pl.semaphore_wait(barrier, met)

    def relay(hop, sub, block, way, to):
        rows = pl.ds(sub * (in_feats // SUBS), in_feats // SUBS)
        part = feats.at[block, rows]
        got = f_rs.at[way, hop - 1, sub] if hop < shards - 1 else far_rs.at[way]
        return copy(feat_hbm.at[rows] if hop == 1 else part, part, f_ss.at[way], got, feat=to)

    def inside(z):
        return (z >= 0) & (z < shards)

    def pass_on(hop, sub, way):
        to = 1 - 2 * way
        pl.when(inside(feat - to * (hop - 1)) & inside(feat + to))(
            lambda: relay(hop, sub, feat - to * (hop - 1), way, feat + to).start())

    def forward(*events):
        for way, hop, sub in events:
            to = 1 - 2 * way

            @pl.when(inside(feat - to * hop) & inside(feat + to))
            def _():
                relay(hop, sub, feat - to * hop, way, feat).wait_recv()
                relay(hop + 1, sub, feat - to * hop, way, feat + to).start()

    def settle(count):
        for way in (0, 1):
            to = 1 - 2 * way

            @pl.when(feat == (shards - 1) * (1 - way))
            def _():
                for hop in hops[:-1][-count:] if count else ():
                    for sub in range(SUBS):
                        relay(hop, sub, feat - to * hop, way, feat).wait_recv()
                if not count:
                    everything(feats.at[feat - to * (shards - 1)], far_rs.at[way])

    hops = range(1, shards)
    queue = sorted(
        ((hop - 1) * SUBS + sub + LAG * way, way, hop, sub) for way in (0, 1) for hop in hops[:-1] for sub in range(SUBS))
    queue = [event[1:] for event in queue]

    def step_on(count):
        forward(*queue[:count])
        del queue[:count]

    for sub in range(SUBS):
        for way in (0, 1):
            pass_on(1, sub, way)

    everything(given, load_sem.at[0])
    for h in range(CHUNKS):
        rows = pl.ds(h * chunk, chunk)
        for d in range(blocks):
            c = given[0, rows, pl.ds(d * BLOCK, BLOCK)]
            own_grad[h, d] = jnp.where(given[1, rows, pl.ds(d * BLOCK, BLOCK)] > 0, c, jnp.zeros_like(c))
    for h in range(CHUNKS):
        for off in range(1, groups):
            copy(own_grad.at[h], grads[h].at[off - 1], out_ss, x_rs.at[h],
                 node=lax.rem(node + off, groups)).start()

    loads[3].wait()
    everything(lists, load_sem.at[3])
    loads[6].wait()
    for g in range(groups):
        s = lax.rem(node - g + groups, groups)
        for t in range(slots):
            count = jnp.full((1, BLOCK), count_ref[s], jnp.int32)
            target = jnp.full((1, BLOCK), lists[1, 0, s, 0, t], jnp.int32)
            tgt[0, pl.ds(g * slots + t, 1), :] = jnp.where(count > t, target, jnp.full_like(target, -1))
    for t in range(slots):
        block = lists[0, 0, node, 0, t]
        picked = jnp.concatenate([own_grad[h, block] for h in range(CHUNKS)], axis=0)
        out = jnp.dot(picked, tiles[0, node, 0, t], preferred_element_type=jnp.float32)
        for h in range(CHUNKS):
            part = out[h * chunk:(h + 1) * chunk]
            own_prod[h, t] = part
            prod_a[0, h, t] = part.astype(jnp.bfloat16)
    for off in range(1, pieces):
        to = lax.rem(rep + off, pieces)
        copy(tgt.at[0], tgt.at[off], out_ss, t_rs, rep=to).start()
        copy(prod_a.at[0], prod_a.at[off], out_ss, a_rs, rep=to).start()

    def other_products(h, off):
        s = lax.rem(node - off + groups, groups)
        for t in range(slots):
            out = jnp.dot(grads[h][off - 1, lists[0, 0, s, 0, t]], tiles[0, s, 0, t],
                          preferred_element_type=jnp.float32)
            own_prod[h, off * slots + t] = out
            prod_b[h, 0, (off - 1) * slots + t] = out.astype(jnp.bfloat16)

    for h in range(CHUNKS):
        step_on(AHEAD[h])
        everything(grads[h], x_rs.at[h])
        if groups <= 4:
            for off in range(1, groups):
                other_products(h, off)
        else:
            lax.fori_loop(1, groups, lambda off, carry, h=h: (other_products(h, off), carry)[1], 0)
        for off in range(1, pieces):
            copy(prod_b.at[h, 0], prod_b.at[h, off], out_ss, b_rs.at[h], rep=lax.rem(rep + off, pieces)).start()

    def add_up(total, from_rep, first, count, read):
        def step(n, total):
            value = read(n).astype(jnp.float32)
            to = tgt[from_rep, pl.ds(first + n, 1), :]
            zero = jnp.zeros_like(value)
            return tuple(
                part + jnp.where(jnp.broadcast_to(to == rep * blocks + d, value.shape), value, zero)
                for d, part in enumerate(total)
            )

        return lax.fori_loop(0, count, step, total, unroll=count <= 8)

    def add_near(h):
        total = tuple(jnp.zeros((chunk, BLOCK), jnp.float32) for _ in range(blocks))
        total = add_up(total, 0, 0, groups * slots, lambda n: own_prod[h, n])
        for off in range(1, pieces):
            total = add_up(total, off, 0, slots, lambda n, off=off: prod_a[off, h, n])
        for d in range(blocks):
            acc[h, d] = total[d]

    step_on(LATER)
    others = pl.ds(1, pieces - 1)
    everything(tgt.at[others], t_rs)
    everything(prod_a.at[others], a_rs)
    for h in range(CHUNKS):
        step_on(NEAR[h] if h < len(NEAR) else 0)
        add_near(h)

    per = cols // BLOCK
    for h in range(CHUNKS):
        everything(prod_b.at[h, pl.ds(1, pieces - 1)], b_rs.at[h])
        total = tuple(acc[h, d] for d in range(blocks))
        for off in range(1, pieces):
            total = add_up(
                total, off, slots, (groups - 1) * slots, lambda n, h=h, off=off: prod_b[h, off, n])
        for d in range(blocks):
            aggs[d // per, pl.ds(h * chunk, chunk), pl.ds((d % per) * BLOCK, BLOCK)] = total[d].astype(jnp.bfloat16)
    agg_all[feat] = aggs[feat]

    step_on(len(queue))
    settle(shards - 2)
    loads[2].wait()
    scale = 1.0 / math.sqrt(piece_len * plane)
    wt = jnp.zeros((width, in_feats), jnp.float32)
    for k in range(shards):
        if k == shards - 1:
            settle(0)
        z = jnp.where(feat < shards // 2, k, shards - 1 - k)
        wt += lax.dot_general(
            aggs[z], feats[z], (((1,), (1,)), ((), ())), preferred_element_type=jnp.float32)
    wt *= scale
    for p in range(parts):
        part = wt[(p // halves) * ROWS:(p // halves + 1) * ROWS, (p % halves) * BLOCK:(p % halves + 1) * BLOCK]
        wt_own[p] = part
        rs_send[p] = part.astype(jnp.bfloat16)

    place = node * pieces + rep

    def to_reducer(q):
        return copy(
            rs_send.at[q], rs_recv.at[lax.rem(place - q + plane, plane)], r_ss, r_rs,
            node=q // pieces, rep=lax.rem(q, pieces))

    if plane == parts and powers:
        for n, r in flips:
            if n or r:
                to_reducer(flip(node, n) * pieces + flip(rep, r)).start()
    elif plane == parts:
        for off in range(1, plane):
            to_reducer(lax.rem(place + off, plane)).start()
    else:
        for q in range(parts):
            @pl.when(place != q)
            def _():
                to_reducer(q).start()

    for off in range(1, shards):
        to = lax.rem(feat + off, shards)
        copy(aggs.at[to], agg_all.at[feat], out_ss, z_rs, feat=to).start()

    def reduce_and_send():
        pltpu.make_async_copy(
            rs_recv.at[pl.ds(1, plane - 1)], rs_recv.at[pl.ds(1, plane - 1)], r_rs).wait()
        total = lax.fori_loop(
            1, plane, lambda j, value: value + rs_recv[j].astype(jnp.float32), wt_own[place],
            unroll=plane <= 8)
        mine = feat * parts + place
        gathered[mine] = total.astype(jnp.bfloat16)

        if powers and devices <= MAX_SENDS:
            for z in range(shards):
                for n, r in flips:
                    def start(z=z, n=n, r=r):
                        copy(gathered.at[mine], gathered.at[mine], g_ss, g_rs,
                             node=flip(node, n), rep=flip(rep, r), feat=z).start()

                    if n or r:
                        start()
                    else:
                        pl.when(feat != z)(start)
            return

        def send(off, carry):
            copy(gathered.at[mine], gathered.at[mine], g_ss, g_rs, **peer_of(off)).start()
            return carry

        lax.fori_loop(1, devices, send, 0)

    if plane == parts:
        reduce_and_send()
    else:
        pl.when(place < parts)(reduce_and_send)

    everything(agg_all.at[pl.ds(0, shards - 1)], z_rs)

    loads[7].wait()
    mixed_ref[...] = jnp.dot(
        weight[...], agg_all[...].reshape(shards * width, cols), preferred_element_type=jnp.float32).astype(jnp.bfloat16)

    for count in hops:
        pl.when(feat == count - 1)(lambda count=count: everything(feats.at[pl.ds(0, count)], f_ss.at[0]))
        pl.when(feat == shards - count)(lambda count=count: everything(feats.at[pl.ds(0, count)], f_ss.at[1]))
    everything(bulk, out_ss)

    def reduced(count):
        everything(rs_send.at[pl.ds(0, count)], r_ss)

    if plane == parts:
        reduced(parts - 1)
    else:
        pl.when(place < parts)(lambda: reduced(parts - 1))
        pl.when(place >= parts)(lambda: reduced(parts))

    def all_but(k):
        pltpu.make_async_copy(gathered.at[pl.ds(0, shards * parts - k)],
                              gathered.at[pl.ds(0, shards * parts - k)], g_rs).wait()

    if plane == parts:
        all_but(1)
    else:
        pl.when(place < parts)(lambda: all_but(1))
        pl.when(place >= parts)(lambda: all_but(0))
    all_ref[...] = gathered[...]

    def drain():
        everything(sent, g_ss)

    if plane == parts:
        drain()
    else:
        pl.when(place < parts)(drain)


def finish(halves, mixed_ref, all_ref, ig_ref, wg_ref):
    ig_ref[...] = mixed_ref[...]
    bands = all_ref.shape[0] // halves
    for half in range(halves):
        side = jnp.concatenate([all_ref[b * halves + half] for b in range(bands)], axis=0)
        wg_ref[pl.ds(half * BLOCK, BLOCK), :] = side.astype(jnp.float32).T


def shards_step(groups, pieces, shards, cotangent, preact, features, weight, tile_values,
                source_blocks, target_blocks, tile_counts):
    width, piece_len = cotangent.shape
    slots = tile_values.shape[3]
    chunk = width // CHUNKS
    blocks = piece_len // BLOCK
    cols = piece_len // shards
    in_feats = features.shape[0]
    per = cols // BLOCK
    plane = groups * pieces
    parts = (width // ROWS) * (in_feats // BLOCK)
    bf16, f32 = jnp.bfloat16, jnp.float32
    dma = pltpu.SemaphoreType.DMA
    out_rows = (groups - 1) * width * blocks + (pieces - 1) * groups * slots * (2 + width) + (shards - 1) * width * per
    hbm = pl.BlockSpec(memory_space=pl.ANY)
    vmem = pl.BlockSpec(memory_space=pltpu.VMEM)
    mixed, everything = pl.pallas_call(
        functools.partial(kernel, groups, pieces, shards),
        out_shape=(
            pltpu.VMEM((weight.shape[0], cols), bf16),
            pltpu.VMEM((shards * parts, ROWS, BLOCK), bf16),
        ),
        in_specs=[hbm] * 8,
        out_specs=(vmem, vmem),
        scratch_shapes=[
            pltpu.VMEM((2, width, piece_len), bf16),
            pltpu.VMEM(tile_values.shape, bf16),
            pltpu.VMEM(weight.shape, bf16),
            pltpu.VMEM((CHUNKS, blocks, chunk, BLOCK), bf16),
            [pltpu.VMEM((groups - 1, blocks, chunk, BLOCK), bf16) for _ in range(CHUNKS)],
            pltpu.VMEM((shards, in_feats, cols), bf16),
            pltpu.VMEM((pieces, groups * slots, BLOCK), jnp.int32),
            pltpu.VMEM((CHUNKS, groups * slots, chunk, BLOCK), f32),
            pltpu.VMEM((pieces, CHUNKS, slots, chunk, BLOCK), bf16),
            pltpu.VMEM((CHUNKS, pieces, (groups - 1) * slots, chunk, BLOCK), bf16),
            pltpu.VMEM((CHUNKS, blocks, chunk, BLOCK), f32),
            pltpu.VMEM((shards, width, cols), bf16),
            pltpu.VMEM((shards, width, cols), bf16),
            pltpu.VMEM((parts, ROWS, BLOCK), f32),
            pltpu.VMEM((parts, ROWS, BLOCK), bf16),
            pltpu.VMEM((plane, ROWS, BLOCK), bf16),
            pltpu.VMEM((groups * pieces * shards - 1, ROWS, BLOCK), bf16),
            pltpu.VMEM((out_rows, BLOCK), bf16),
            pltpu.VMEM((shards * parts, ROWS, BLOCK), bf16),
            pltpu.SMEM((2, *source_blocks.shape), jnp.int32),
            pltpu.SMEM((groups,), jnp.int32),
            dma((6,)),
            dma(()), dma((CHUNKS,)),
            dma((2,)), dma((2, max(shards - 2, 1), SUBS)), dma((2,)),
            dma(()), dma(()), dma((CHUNKS,)), dma(()),
            dma(()), dma(()),
            dma(()), dma(()),
        ],
        compiler_params=pltpu.CompilerParams(collective_id=0, has_side_effects=True, vmem_limit_bytes=40 * 2**20),
        name="graph_backward",
    )(*(pltpu.with_memory_space_constraint(a, pltpu.HBM) for a in (
        cotangent, preact, features, tile_values, source_blocks, target_blocks, tile_counts.reshape(groups), weight)))
    return pl.pallas_call(
        functools.partial(finish, in_feats // BLOCK),
        out_shape=(
            jax.ShapeDtypeStruct((weight.shape[0], cols), bf16),
            jax.ShapeDtypeStruct((in_feats, width * shards), f32),
        ),
        in_specs=[vmem] * 2,
        out_specs=(vmem, vmem),
        name="finish",
        compiler_params=pltpu.CompilerParams(vmem_limit_bytes=16 * 2**20),
    )(pltpu.with_memory_space_constraint(mixed, pltpu.VMEM), pltpu.with_memory_space_constraint(everything, pltpu.VMEM))


def solution(mesh):
    step = functools.partial(shards_step, mesh.shape["node"], mesh.shape["rep"], mesh.shape["feat"])
    in_specs = (
        P("feat", ("node", "rep")),
        P("feat", ("node", "rep")),
        P(None, ("node", "rep", "feat")),
        P(),
        P("node", None, "rep", None, None, None),
        P("node", None, "rep", None),
        P("node", None, "rep", None),
        P("node", None, "rep"),
    )
    out_specs = (P(None, ("node", "rep", "feat")), P())
    return jax.shard_map(step, mesh=mesh, in_specs=in_specs, out_specs=out_specs, check_vma=False)
```

```python
import functools
import math

import jax
import jax.numpy as jnp
from jax import lax
from jax.experimental import pallas as pl
from jax.experimental.pallas import tpu as pltpu
from jax.sharding import PartitionSpec as P

MESH = pl.DeviceIdType.MESH
BLOCK = 128
CHUNKS = 4
ROWS = 16
SUBS = 4
LAG = 0
AHEAD = (3, 2, 2, 2)
LATER = 3
NEAR = (2, 1, 1)
MAX_SENDS = 32


def kernel(
    groups, pieces, shards,
    cot_hbm, pre_hbm, feat_hbm, tiles_hbm, source_hbm, target_hbm, count_hbm, weight_hbm,
    mixed_ref, all_ref,
    given, tiles, weight, own_grad, grads, feats, tgt, own_prod, prod_a, prod_b, acc, aggs, agg_all,
    wt_own, rs_send, rs_recv, sent, bulk, gathered, lists, count_ref,
    load_sem, out_ss, x_rs, f_ss, f_rs, far_rs, t_rs, a_rs, b_rs, z_rs, r_ss, r_rs, g_ss, g_rs,
):
    node = lax.axis_index("node")
    rep = lax.axis_index("rep")
    feat = lax.axis_index("feat")
    devices = groups * pieces * shards
    plane = groups * pieces
    me = (node * pieces + rep) * shards + feat
    slots = tiles_hbm.shape[3]
    width, piece_len = given.shape[1:]
    chunk = width // CHUNKS
    blocks = piece_len // BLOCK
    cols = piece_len // shards
    in_feats = feats.shape[1]
    halves = in_feats // BLOCK
    parts = (width // ROWS) * halves

    def copy(src, dst, ss, rs, **where):
        where = {"node": node, "rep": rep, "feat": feat, **where}
        return pltpu.make_async_remote_copy(
            src_ref=src, dst_ref=dst, send_sem=ss, recv_sem=rs, device_id=where, device_id_type=MESH
        )

    def flip(index, mask):
        bit = 1
        while bit <= mask:
            if mask & bit:
                index = index + bit * (1 - 2 * lax.rem(index // bit, 2))
            bit *= 2
        return index

    powers = all(n & (n - 1) == 0 for n in (groups, pieces))
    flips = sorted(
        ((n, r) for n in range(groups) for r in range(pieces)), key=lambda f: -(f[0] > 0) - (f[1] > 1))

    def peer_of(off):
        peer = lax.rem(me + off, devices)
        return {
            "node": peer // (pieces * shards),
            "rep": lax.rem(peer // shards, pieces),
            "feat": lax.rem(peer, shards),
        }

    def everything(ref, sem):
        pltpu.make_async_copy(ref, ref, sem).wait()

    barrier = pltpu.get_barrier_semaphore()

    def greet(**where):
        where = {"node": node, "rep": rep, "feat": feat, **where}
        pl.semaphore_signal(barrier, inc=1, device_id=where, device_id_type=MESH)

    for off in range(1, groups):
        greet(node=lax.rem(node + off, groups))
    for off in range(1, pieces):
        greet(rep=lax.rem(rep + off, pieces))
    met = groups + pieces - 2
    for to in (1, -1):
        pl.when((feat + to >= 0) & (feat + to < shards))(lambda to=to: greet(feat=feat + to))
        met += jnp.where((feat + to >= 0) & (feat + to < shards), 1, 0)

    loads = [
        pltpu.make_async_copy(cot_hbm, given.at[0], load_sem.at[0]),
        pltpu.make_async_copy(pre_hbm, given.at[1], load_sem.at[0]),
        pltpu.make_async_copy(feat_hbm, feats.at[feat], load_sem.at[1]),
        pltpu.make_async_copy(tiles_hbm, tiles, load_sem.at[2]),
        pltpu.make_async_copy(source_hbm, lists.at[0], load_sem.at[3]),
        pltpu.make_async_copy(target_hbm, lists.at[1], load_sem.at[3]),
        pltpu.make_async_copy(count_hbm, count_ref, load_sem.at[4]),
        pltpu.make_async_copy(weight_hbm, weight, load_sem.at[5]),
    ]
    for load in loads:
        load.start()
    pl.semaphore_wait(barrier, met)

    def relay(hop, sub, block, way, to):
        rows = pl.ds(sub * (in_feats // SUBS), in_feats // SUBS)
        part = feats.at[block, rows]
        got = f_rs.at[way, hop - 1, sub] if hop < shards - 1 else far_rs.at[way]
        return copy(part, part, f_ss.at[way], got, feat=to)

    def inside(z):
        return (z >= 0) & (z < shards)

    def pass_on(hop, sub, way):
        to = 1 - 2 * way
        pl.when(inside(feat - to * (hop - 1)) & inside(feat + to))(
            lambda: relay(hop, sub, feat - to * (hop - 1), way, feat + to).start())

    def forward(*events):
        for way, hop, sub in events:
            to = 1 - 2 * way

            @pl.when(inside(feat - to * hop) & inside(feat + to))
            def _():
                relay(hop, sub, feat - to * hop, way, feat).wait_recv()
                relay(hop + 1, sub, feat - to * hop, way, feat + to).start()

    def settle(count):
        for way in (0, 1):
            to = 1 - 2 * way

            @pl.when(feat == (shards - 1) * (1 - way))
            def _():
                for hop in hops[:-1][-count:] if count else ():
                    for sub in range(SUBS):
                        relay(hop, sub, feat - to * hop, way, feat).wait_recv()
                if not count:
                    everything(feats.at[feat - to * (shards - 1)], far_rs.at[way])

    hops = range(1, shards)
    queue = sorted(
        ((hop - 1) * SUBS + sub + LAG * way, way, hop, sub) for way in (0, 1) for hop in hops[:-1] for sub in range(SUBS))
    queue = [event[1:] for event in queue]

    def step_on(count):
        forward(*queue[:count])
        del queue[:count]

    loads[2].wait()
    for sub in range(SUBS):
        for way in (0, 1):
            pass_on(1, sub, way)

    everything(given, load_sem.at[0])
    for h in range(CHUNKS):
        rows = pl.ds(h * chunk, chunk)
        for d in range(blocks):
            c = given[0, rows, pl.ds(d * BLOCK, BLOCK)]
            own_grad[h, d] = jnp.where(given[1, rows, pl.ds(d * BLOCK, BLOCK)] > 0, c, jnp.zeros_like(c))
    for h in range(CHUNKS):
        for off in range(1, groups):
            copy(own_grad.at[h], grads[h].at[off - 1], out_ss, x_rs.at[h],
                 node=lax.rem(node + off, groups)).start()

    loads[3].wait()
    everything(lists, load_sem.at[3])
    loads[6].wait()
    for g in range(groups):
        s = lax.rem(node - g + groups, groups)
        for t in range(slots):
            count = jnp.full((1, BLOCK), count_ref[s], jnp.int32)
            target = jnp.full((1, BLOCK), lists[1, 0, s, 0, t], jnp.int32)
            tgt[0, pl.ds(g * slots + t, 1), :] = jnp.where(count > t, target, jnp.full_like(target, -1))
    for t in range(slots):
        block = lists[0, 0, node, 0, t]
        picked = jnp.concatenate([own_grad[h, block] for h in range(CHUNKS)], axis=0)
        out = jnp.dot(picked, tiles[0, node, 0, t], preferred_element_type=jnp.float32)
        for h in range(CHUNKS):
            part = out[h * chunk:(h + 1) * chunk]
            own_prod[h, t] = part
            prod_a[0, h, t] = part.astype(jnp.bfloat16)
    for off in range(1, pieces):
        to = lax.rem(rep + off, pieces)
        copy(tgt.at[0], tgt.at[off], out_ss, t_rs, rep=to).start()
        copy(prod_a.at[0], prod_a.at[off], out_ss, a_rs, rep=to).start()

    def other_products(h, off):
        s = lax.rem(node - off + groups, groups)
        for t in range(slots):
            out = jnp.dot(grads[h][off - 1, lists[0, 0, s, 0, t]], tiles[0, s, 0, t],
                          preferred_element_type=jnp.float32)
            own_prod[h, off * slots + t] = out
            prod_b[h, 0, (off - 1) * slots + t] = out.astype(jnp.bfloat16)

    for h in range(CHUNKS):
        step_on(AHEAD[h])
        everything(grads[h], x_rs.at[h])
        if groups <= 4:
            for off in range(1, groups):
                other_products(h, off)
        else:
            lax.fori_loop(1, groups, lambda off, carry, h=h: (other_products(h, off), carry)[1], 0)
        for off in range(1, pieces):
            copy(prod_b.at[h, 0], prod_b.at[h, off], out_ss, b_rs.at[h], rep=lax.rem(rep + off, pieces)).start()

    def add_up(total, from_rep, first, count, read):
        def step(n, total):
            value = read(n).astype(jnp.float32)
            to = tgt[from_rep, pl.ds(first + n, 1), :]
            zero = jnp.zeros_like(value)
            return tuple(
                part + jnp.where(jnp.broadcast_to(to == rep * blocks + d, value.shape), value, zero)
                for d, part in enumerate(total)
            )

        return lax.fori_loop(0, count, step, total, unroll=count <= 8)

    def add_near(h):
        total = tuple(jnp.zeros((chunk, BLOCK), jnp.float32) for _ in range(blocks))
        total = add_up(total, 0, 0, groups * slots, lambda n: own_prod[h, n])
        for off in range(1, pieces):
            total = add_up(total, off, 0, slots, lambda n, off=off: prod_a[off, h, n])
        for d in range(blocks):
            acc[h, d] = total[d]

    step_on(LATER)
    others = pl.ds(1, pieces - 1)
    everything(tgt.at[others], t_rs)
    everything(prod_a.at[others], a_rs)
    for h in range(CHUNKS):
        step_on(NEAR[h] if h < len(NEAR) else 0)
        add_near(h)

    per = cols // BLOCK
    for h in range(CHUNKS):
        everything(prod_b.at[h, pl.ds(1, pieces - 1)], b_rs.at[h])
        total = tuple(acc[h, d] for d in range(blocks))
        for off in range(1, pieces):
            total = add_up(
                total, off, slots, (groups - 1) * slots, lambda n, h=h, off=off: prod_b[h, off, n])
        for d in range(blocks):
            aggs[d // per, pl.ds(h * chunk, chunk), pl.ds((d % per) * BLOCK, BLOCK)] = total[d].astype(jnp.bfloat16)
    agg_all[feat] = aggs[feat]

    step_on(len(queue))
    settle(shards - 2)
    scale = 1.0 / math.sqrt(piece_len * plane)
    wt = jnp.zeros((width, in_feats), jnp.float32)
    for k in range(shards):
        if k == shards - 1:
            settle(0)
        z = jnp.where(feat < shards // 2, k, shards - 1 - k)
        wt += lax.dot_general(
            aggs[z], feats[z], (((1,), (1,)), ((), ())), preferred_element_type=jnp.float32)
    wt *= scale
    for p in range(parts):
        part = wt[(p // halves) * ROWS:(p // halves + 1) * ROWS, (p % halves) * BLOCK:(p % halves + 1) * BLOCK]
        rs_send[p] = part.astype(jnp.bfloat16)

    place = node * pieces + rep

    def to_reducer(q):
        return copy(
            rs_send.at[q], rs_recv.at[lax.rem(place - q + plane, plane)], r_ss, r_rs,
            node=q // pieces, rep=lax.rem(q, pieces))

    if plane == parts and powers:
        for n, r in flips:
            if n or r:
                to_reducer(flip(node, n) * pieces + flip(rep, r)).start()
    elif plane == parts:
        for off in range(1, plane):
            to_reducer(lax.rem(place + off, plane)).start()
    else:
        for q in range(parts):
            @pl.when(place != q)
            def _():
                to_reducer(q).start()

    for p in range(parts):
        wt_own[p] = wt[(p // halves) * ROWS:(p // halves + 1) * ROWS, (p % halves) * BLOCK:(p % halves + 1) * BLOCK]

    for off in range(1, shards):
        to = lax.rem(feat + off, shards)
        copy(aggs.at[to], agg_all.at[feat], out_ss, z_rs, feat=to).start()

    def reduce_and_send():
        pltpu.make_async_copy(
            rs_recv.at[pl.ds(1, plane - 1)], rs_recv.at[pl.ds(1, plane - 1)], r_rs).wait()
        total = lax.fori_loop(
            1, plane, lambda j, value: value + rs_recv[j].astype(jnp.float32), wt_own[place],
            unroll=plane <= 8)
        mine = feat * parts + place
        gathered[mine] = total.astype(jnp.bfloat16)

        if powers and devices <= MAX_SENDS:
            for z in range(shards):
                for n, r in flips:
                    def start(z=z, n=n, r=r):
                        copy(gathered.at[mine], gathered.at[mine], g_ss, g_rs,
                             node=flip(node, n), rep=flip(rep, r), feat=z).start()

                    if n or r:
                        start()
                    else:
                        pl.when(feat != z)(start)
            return

        def send(off, carry):
            copy(gathered.at[mine], gathered.at[mine], g_ss, g_rs, **peer_of(off)).start()
            return carry

        lax.fori_loop(1, devices, send, 0)

    if plane == parts:
        reduce_and_send()
    else:
        pl.when(place < parts)(reduce_and_send)

    everything(agg_all.at[pl.ds(0, shards - 1)], z_rs)

    loads[7].wait()
    mixed_ref[...] = jnp.dot(
        weight[...], agg_all[...].reshape(shards * width, cols), preferred_element_type=jnp.float32).astype(jnp.bfloat16)

    for count in hops:
        pl.when(feat == count - 1)(lambda count=count: everything(feats.at[pl.ds(0, count)], f_ss.at[0]))
        pl.when(feat == shards - count)(lambda count=count: everything(feats.at[pl.ds(0, count)], f_ss.at[1]))
    everything(bulk, out_ss)

    def reduced(count):
        everything(rs_send.at[pl.ds(0, count)], r_ss)

    if plane == parts:
        reduced(parts - 1)
    else:
        pl.when(place < parts)(lambda: reduced(parts - 1))
        pl.when(place >= parts)(lambda: reduced(parts))

    def all_but(k):
        pltpu.make_async_copy(gathered.at[pl.ds(0, shards * parts - k)],
                              gathered.at[pl.ds(0, shards * parts - k)], g_rs).wait()

    if plane == parts:
        all_but(1)
    else:
        pl.when(place < parts)(lambda: all_but(1))
        pl.when(place >= parts)(lambda: all_but(0))
    all_ref[...] = gathered[...]

    def drain():
        everything(sent, g_ss)

    if plane == parts:
        drain()
    else:
        pl.when(place < parts)(drain)


def finish(halves, mixed_ref, all_ref, ig_ref, wg_ref):
    ig_ref[...] = mixed_ref[...]
    bands = all_ref.shape[0] // halves
    for half in range(halves):
        side = jnp.concatenate([all_ref[b * halves + half] for b in range(bands)], axis=0)
        wg_ref[pl.ds(half * BLOCK, BLOCK), :] = side.astype(jnp.float32).T


def shards_step(groups, pieces, shards, cotangent, preact, features, weight, tile_values,
                source_blocks, target_blocks, tile_counts):
    width, piece_len = cotangent.shape
    slots = tile_values.shape[3]
    chunk = width // CHUNKS
    blocks = piece_len // BLOCK
    cols = piece_len // shards
    in_feats = features.shape[0]
    per = cols // BLOCK
    plane = groups * pieces
    parts = (width // ROWS) * (in_feats // BLOCK)
    bf16, f32 = jnp.bfloat16, jnp.float32
    dma = pltpu.SemaphoreType.DMA
    out_rows = (groups - 1) * width * blocks + (pieces - 1) * groups * slots * (2 + width) + (shards - 1) * width * per
    hbm = pl.BlockSpec(memory_space=pl.ANY)
    vmem = pl.BlockSpec(memory_space=pltpu.VMEM)
    mixed, everything = pl.pallas_call(
        functools.partial(kernel, groups, pieces, shards),
        out_shape=(
            pltpu.VMEM((weight.shape[0], cols), bf16),
            pltpu.VMEM((shards * parts, ROWS, BLOCK), bf16),
        ),
        in_specs=[hbm] * 8,
        out_specs=(vmem, vmem),
        scratch_shapes=[
            pltpu.VMEM((2, width, piece_len), bf16),
            pltpu.VMEM(tile_values.shape, bf16),
            pltpu.VMEM(weight.shape, bf16),
            pltpu.VMEM((CHUNKS, blocks, chunk, BLOCK), bf16),
            [pltpu.VMEM((groups - 1, blocks, chunk, BLOCK), bf16) for _ in range(CHUNKS)],
            pltpu.VMEM((shards, in_feats, cols), bf16),
            pltpu.VMEM((pieces, groups * slots, BLOCK), jnp.int32),
            pltpu.VMEM((CHUNKS, groups * slots, chunk, BLOCK), f32),
            pltpu.VMEM((pieces, CHUNKS, slots, chunk, BLOCK), bf16),
            pltpu.VMEM((CHUNKS, pieces, (groups - 1) * slots, chunk, BLOCK), bf16),
            pltpu.VMEM((CHUNKS, blocks, chunk, BLOCK), f32),
            pltpu.VMEM((shards, width, cols), bf16),
            pltpu.VMEM((shards, width, cols), bf16),
            pltpu.VMEM((parts, ROWS, BLOCK), f32),
            pltpu.VMEM((parts, ROWS, BLOCK), bf16),
            pltpu.VMEM((plane, ROWS, BLOCK), bf16),
            pltpu.VMEM((groups * pieces * shards - 1, ROWS, BLOCK), bf16),
            pltpu.VMEM((out_rows, BLOCK), bf16),
            pltpu.VMEM((shards * parts, ROWS, BLOCK), bf16),
            pltpu.SMEM((2, *source_blocks.shape), jnp.int32),
            pltpu.SMEM((groups,), jnp.int32),
            dma((6,)),
            dma(()), dma((CHUNKS,)),
            dma((2,)), dma((2, max(shards - 2, 1), SUBS)), dma((2,)),
            dma(()), dma(()), dma((CHUNKS,)), dma(()),
            dma(()), dma(()),
            dma(()), dma(()),
        ],
        compiler_params=pltpu.CompilerParams(collective_id=0, has_side_effects=True, vmem_limit_bytes=40 * 2**20),
        name="graph_backward",
    )(*(pltpu.with_memory_space_constraint(a, pltpu.HBM) for a in (
        cotangent, preact, features, tile_values, source_blocks, target_blocks, tile_counts.reshape(groups), weight)))
    return pl.pallas_call(
        functools.partial(finish, in_feats // BLOCK),
        out_shape=(
            jax.ShapeDtypeStruct((weight.shape[0], cols), bf16),
            jax.ShapeDtypeStruct((in_feats, width * shards), f32),
        ),
        in_specs=[vmem] * 2,
        out_specs=(vmem, vmem),
        name="finish",
        compiler_params=pltpu.CompilerParams(vmem_limit_bytes=16 * 2**20),
    )(pltpu.with_memory_space_constraint(mixed, pltpu.VMEM), pltpu.with_memory_space_constraint(everything, pltpu.VMEM))


def solution(mesh):
    step = functools.partial(shards_step, mesh.shape["node"], mesh.shape["rep"], mesh.shape["feat"])
    in_specs = (
        P("feat", ("node", "rep")),
        P("feat", ("node", "rep")),
        P(None, ("node", "rep", "feat")),
        P(),
        P("node", None, "rep", None, None, None),
        P("node", None, "rep", None),
        P("node", None, "rep", None),
        P("node", None, "rep"),
    )
    out_specs = (P(None, ("node", "rep", "feat")), P())
    return jax.shard_map(step, mesh=mesh, in_specs=in_specs, out_specs=out_specs, check_vma=False)
```
